32 devices in a mesh: rep: 16 (over z, y, core), shard: 2 (over x).
Axes of the slice: x: 2, y: 2, z: 4, core: 2. Of those that a mesh axis runs over, the one named last changes fastest.
Arguments:
- tokens: bfloat16 [4096, 1024], P(('rep', 'shard')), may hold values from -6 to 6
- positions: int32 [4096], P(('rep', 'shard')), may hold values from 0 to 381, as said below
- routes: int32 [4096, 2], P(('rep', 'shard')), may hold values from 0 to 7, all different within a row; in each aligned block of 128 rows (0 to 127, 128 to 255, ...) at most 48 rows name the same one
- gates: float32 [4096, 2], P(('rep', 'shard')), may hold values from 0.1 to 1
- cotangent: bfloat16 [4096, 1024], P(('rep', 'shard')), may hold values from -6 to 6
- attn_gain: bfloat16 [1024], P('shard'), may hold values from 0.5 to 1.5
- w_query: bfloat16 [1024, 1024], P('shard'), may hold values from -0.75 to 0.75
- key_weight: bfloat16 [1024, 512], P('shard'), may hold values from -0.75 to 0.75
- value_weight: bfloat16 [1024, 512], P('shard'), may hold values from -0.1875 to 0.1875
- w_out: bfloat16 [1024, 1024], P('shard'), may hold values from -3 to 3
- ffn_gain: bfloat16 [1024], P('shard'), may hold values from 0.5 to 1.5
- w_gate_up: bfloat16 [8, 1024, 1024], P('shard'), may hold values from -0.1875 to 0.1875
- w_down: bfloat16 [8, 512, 1024], P('shard'), may hold values from -1.5 to 1.5
Outputs:
- output: bfloat16 [4096, 1024], P(('rep', 'shard'))
- input_grad: bfloat16 [4096, 1024], P(('rep', 'shard'))
- grad_attn_gain: float32 [1024], P('shard')
- grad_w_query: float32 [1024, 1024], P('shard')
- grad_w_key: float32 [1024, 512], P('shard')
- grad_w_value: float32 [1024, 512], P('shard')
- grad_w_out: float32 [1024, 1024], P('shard')
- grad_ffn_gain: float32 [1024], P('shard')
- grad_w_gate_up: float32 [8, 1024, 1024], P('shard')
- grad_w_down: float32 [8, 512, 1024], P('shard')
The draws below stay inside these ranges and needn't reach their ends.
Inputs may be any that keep to these rules, and one draw needn't show every extreme that they name: Within each sequence of 128 tokens positions start at 0 and rise by 1, 2 or 3 from token to token; in one sequence they rise by 3 at every token. `routes`: among the rows of one device no expert is named more than 48 times.
All inputs are finite; a program needn't handle non-finite values.
Results may differ from the reference program's by a relative error of at most 0.023.
Values may be sent and summed in bfloat16 or wider, within the bound.
No kernel may reach another device: no remote copies, remote signals or barrier semaphores. Data moves between devices by JAX's collectives and lax.ppermute only.
A program may use at most 192 MiB of HBM per device.

```python
import math
import jax
import jax.numpy as jnp
import numpy as np
from jax import lax

MODEL_DIM = 1024
QUERY_HEADS = 16
KEY_VALUE_HEADS = 8
HEAD_DIM = 64
F = 512
EXPERTS = 8
TOP = 2
SEQUENCE_TOKENS = 128
CAP = 48
TOKENS = 4096
N_SHARD = 2


def draw_positions(key, part):
    sequences = TOKENS // SEQUENCE_TOKENS
    steps_drawn = jax.random.randint(jax.random.fold_in(key, 1), (sequences, SEQUENCE_TOKENS), 1, 4, dtype=jnp.int32)
    chosen = jax.random.randint(jax.random.fold_in(key, 2), (), 0, sequences, dtype=jnp.int32)
    is_chosen = (jnp.arange(sequences, dtype=jnp.int32) == chosen)[:, None]
    steps_drawn = jnp.where(is_chosen, jnp.int32(3), steps_drawn).astype(jnp.int32)
    rising = jnp.cumsum(steps_drawn, axis=1) - steps_drawn[:, :1]
    return rising.reshape(TOKENS).astype(jnp.int32)


def steps_of(rng, dims, shards, low, largest):
    def one(dim, shards_of):
        steps = jax.random.uniform(jax.random.fold_in(jax.random.fold_in(rng, 6), dim), (shards_of,), jnp.float32, low / len(shards), largest / len(shards))
        return jnp.repeat(jnp.exp(steps), dims[dim] // shards_of).reshape((-1,) + (1,) * (len(dims) - dim - 1))

    level = one(*shards[0])
    for cut in shards[1:]:
        level = level * one(*cut)
    return level


def shared_out(stream_key, own, number, rows, count, top, reach, lean):
    order = jax.random.permutation(stream_key, count)
    heavy_load, ordinary = load_shares(count, rows * top, reach, lean, True), load_shares(count, rows * top, reach, lean, False)
    places = jnp.arange(count)

    def named(sizes, offset_by):
        used = int((sizes > 0).sum())
        fixed = max(1, used // 4)
        moved = fixed + (places - fixed + offset_by * (used - fixed)) % max(1, count - fixed)
        return jnp.zeros((count,), jnp.int32).at[order[jnp.where(places < fixed, places, moved)]].set(jnp.asarray(sizes, jnp.int32))

    sizes = jnp.where(number % 4 == 0, named(heavy_load, number // 4), named(ordinary, number - number // 4 - 1))
    mixed = jax.random.permutation(jax.random.fold_in(own, 3), count)
    giver, taker = mixed[0:count // 2 * 2:2], mixed[1:count // 2 * 2:2]
    margin = jnp.minimum(sizes[giver] - 1, reach - sizes[taker]) // 2
    margin = jnp.where((giver == order[0]) | (taker == order[0]) | (sizes[taker] == 0), 0, jnp.maximum(margin, 0))
    moved = jax.random.randint(jax.random.fold_in(own, 4), (count // 2,), 0, 1 << 20) % (margin + 1)
    sizes = sizes.at[giver].add(-moved).at[taker].add(moved)
    members = jnp.searchsorted(jnp.cumsum(sizes), jnp.arange(rows * top), side="right").astype(jnp.int32)
    table = members.reshape(top, rows).T
    table = table[jax.random.permutation(jax.random.fold_in(own, 1), rows)]
    offset_by = jax.random.randint(jax.random.fold_in(own, 2), (rows, 1), 0, top)
    return jnp.take_along_axis(table, (jnp.arange(top)[None, :] + offset_by) % top, axis=1)


def load_shares(amount, total, bound, lean, full):
    loads = [(1 << 20) // math.isqrt(rank ** lean) + 1 for rank in range(1, amount + 1)]
    largest = bound if full else min(bound, max(-(-total // amount), total * loads[0] // sum(loads)))
    least = 1 if total - largest >= amount - 1 else 0
    counts, rest = [largest] + [least] * (amount - 1), total - largest - least * (amount - 1)
    while rest > 0:
        free = [i for i in range(1, amount) if counts[i] < largest] or [i for i in range(1, amount) if counts[i] < bound]
        pool, budget = sum([loads[i] for i in free]), rest
        for i in free:
            more = min(bound - counts[i], max(1, budget * loads[i] // pool), rest)
            counts[i] = counts[i] + more
            rest = rest - more
    return np.array(counts)


def scatter_about(rng, shape, spread, reach, split=(), held_as=jnp.bfloat16):
    values = spread * jax.random.normal(rng, shape, jnp.float32)
    if split:
        values = values * steps_of(rng, shape, split, -0.22, 0.18)
    return jnp.clip(values, -reach, reach).astype(held_as)


def setup_inputs(seed: int = 0) -> dict:
    seeds = jax.random.split(jax.random.key(seed), 14)
    tokens = scatter_about(seeds[0], (TOKENS, MODEL_DIM), 1.0, 6.0, ((0, 32),))
    positions = draw_positions(jax.random.fold_in(seeds[13], 71), 0)
    routes_keys = jax.random.split(jax.random.fold_in(seeds[2], 1), TOKENS // SEQUENCE_TOKENS)
    routes_turns = jax.random.permutation(jax.random.fold_in(seeds[2], 3), TOKENS // SEQUENCE_TOKENS)
    routes = jax.vmap(lambda own, number: shared_out(jax.random.fold_in(seeds[2], 2), own, number, SEQUENCE_TOKENS, EXPERTS, TOP, CAP, 1))(routes_keys, routes_turns).reshape((TOKENS, TOP))
    gates = jnp.clip(0.1 + 0.9 * jax.random.uniform(seeds[3], (TOKENS, TOP), jnp.float32) ** steps_of(seeds[3], (TOKENS, TOP), ((0, 32),), -0.2, 0.2), 0.1, 1.0)
    cotangent = scatter_about(seeds[4], (TOKENS, MODEL_DIM), 1.0, 6.0, ((0, 32),))
    attn_gain = jnp.clip(1.0 + 0.1 * jax.random.normal(seeds[5], (MODEL_DIM,), jnp.float32), 0.5, 1.5).astype(jnp.bfloat16)
    w_query = scatter_about(seeds[6], (MODEL_DIM, QUERY_HEADS * HEAD_DIM), (MODEL_DIM // 16) ** -0.5, 0.75, ((0, 2),))
    key_weight = scatter_about(seeds[7], (MODEL_DIM, KEY_VALUE_HEADS * HEAD_DIM), (MODEL_DIM // 16) ** -0.5, 0.75, ((0, 2),))
    value_weight = scatter_about(seeds[8], (MODEL_DIM, KEY_VALUE_HEADS * HEAD_DIM), MODEL_DIM ** -0.5, 0.1875, ((0, 2),))
    w_out = scatter_about(seeds[9], (QUERY_HEADS * HEAD_DIM, MODEL_DIM), 4 ** -0.5, 3.0, ((0, 2),))
    ffn_gain = jnp.clip(1.0 + 0.1 * jax.random.normal(seeds[10], (MODEL_DIM,), jnp.float32), 0.5, 1.5).astype(jnp.bfloat16)
    w_gate_up = scatter_about(seeds[11], (EXPERTS, MODEL_DIM, 2 * F), MODEL_DIM ** -0.5, 0.1875, ((0, 2),))
    w_down = scatter_about(seeds[12], (EXPERTS, F, MODEL_DIM), (F // 32) ** -0.5, 1.5, ((0, 2),))
    return {"tokens": tokens, "positions": positions, "routes": routes, "gates": gates, "cotangent": cotangent, "attn_gain": attn_gain, "w_query": w_query, "key_weight": key_weight, "value_weight": value_weight, "w_out": w_out, "ffn_gain": ffn_gain, "w_gate_up": w_gate_up, "w_down": w_down}


RMS_EPS = 1e-06
RES_MULT = 0.22
ATT_MULT = 0.015625
ROPE_BASE = 10000.0
FULL_PRECISION = lax.Precision.HIGHEST

@jax.custom_vjp
def lowered_input(v):
    return lax.optimization_barrier(v.astype(jnp.bfloat16)).astype(jnp.float32)

@jax.custom_vjp
def lowered_gradient(v):
    return v

def low_keep(v):
    return (lowered_input(v), None)

def low_pass(kept, grad):
    return (grad,)

def back_keep(v):
    return (v, None)

def back_low(kept, grad):
    return (lowered_input(grad),)
lowered_input.defvjp(low_keep, low_pass)
lowered_gradient.defvjp(back_keep, back_low)

def rms_norm(values, norm_gain):
    inverse = lax.rsqrt(lax.optimization_barrier(jnp.mean(values * values, axis=-1, keepdims=True)) + RMS_EPS)
    return values * inverse * norm_gain

def rope_tables(positions):
    half_dim = HEAD_DIM // 2
    frequency = ROPE_BASE ** (-(2.0 * jnp.arange(half_dim, dtype=jnp.float32)) / HEAD_DIM)
    angles = positions.astype(jnp.float32)[:, None] * frequency[None, :]
    return (jnp.cos(angles)[:, None, :], jnp.sin(angles)[:, None, :])

def apply_rotary(values, cosine_table, sinusoid_table):
    half_dim = values.shape[-1] // 2
    front_half = values[..., :half_dim]
    back_half = values[..., half_dim:]
    return jnp.concatenate([front_half * cosine_table - back_half * sinusoid_table, back_half * cosine_table + front_half * sinusoid_table], axis=-1)

def swiglu(gate_up):
    return jax.nn.silu(gate_up[..., :F]) * gate_up[..., F:]

def slot_table(routes):
    flat_routes = routes.reshape(-1).astype(jnp.int32)
    onehot = (flat_routes[:, None] == jnp.arange(EXPERTS, dtype=jnp.int32)[None, :]).astype(jnp.int32)
    before = (jnp.cumsum(onehot, axis=0) - onehot).astype(jnp.int32)
    ranked = lax.optimization_barrier(jnp.sum(before * onehot, axis=1)).astype(jnp.int32)
    slot_index = (flat_routes * CAP + ranked).astype(jnp.int32)
    owners = (jnp.arange(flat_routes.shape[0], dtype=jnp.int32) // TOP).astype(jnp.int32)
    sources = jnp.zeros((EXPERTS * CAP,), jnp.int32).at[slot_index].set(owners)
    filled = jnp.zeros((EXPERTS * CAP,), jnp.float32).at[slot_index].set(1.0)
    return (slot_index, sources, filled)

def layer(tokens, positions, routes, gates, attn_gain, w_query, key_weight, value_weight, w_out, ffn_gain, w_gate_up, w_down):
    cosine_table, sinusoid_table = rope_tables(positions)
    normalized_input = lowered_input(rms_norm(tokens, attn_gain))
    query_head_rows = lowered_input(apply_rotary(lowered_gradient(jnp.dot(normalized_input, w_query, precision=FULL_PRECISION)).reshape(SEQUENCE_TOKENS, QUERY_HEADS, HEAD_DIM), cosine_table, sinusoid_table))
    key_head_rows = lowered_input(apply_rotary(lowered_gradient(jnp.dot(normalized_input, key_weight, precision=FULL_PRECISION)).reshape(SEQUENCE_TOKENS, KEY_VALUE_HEADS, HEAD_DIM), cosine_table, sinusoid_table))
    value_head_rows = lowered_gradient(lowered_input(jnp.dot(normalized_input, value_weight, precision=FULL_PRECISION))).reshape(SEQUENCE_TOKENS, KEY_VALUE_HEADS, HEAD_DIM)
    grouped_heads = query_head_rows.reshape(SEQUENCE_TOKENS, KEY_VALUE_HEADS, QUERY_HEADS // KEY_VALUE_HEADS, HEAD_DIM)
    scores = lowered_gradient(ATT_MULT * jnp.einsum('qhgd,khd->hgqk', grouped_heads, key_head_rows, precision=FULL_PRECISION))
    causal = jnp.arange(SEQUENCE_TOKENS)[:, None] >= jnp.arange(SEQUENCE_TOKENS)[None, :]
    weights = jax.nn.softmax(jnp.where(causal, scores, -1e+30), axis=-1)
    attended = jnp.einsum('hgqk,khd->qhgd', lowered_input(weights), value_head_rows, precision=FULL_PRECISION).reshape(SEQUENCE_TOKENS, QUERY_HEADS * HEAD_DIM)
    attended = lowered_gradient(lowered_input(attended))
    branch = lowered_gradient(jnp.dot(attended, w_out, precision=FULL_PRECISION))
    hidden = tokens + RES_MULT * branch
    slot_index, sources, filled = slot_table(routes)
    second = lowered_input(rms_norm(hidden, ffn_gain))
    dispatched = lowered_gradient(second[sources] * filled[:, None]).reshape(EXPERTS, CAP, MODEL_DIM)
    gate_up = lowered_gradient(jnp.einsum('ecd,edf->ecf', dispatched, w_gate_up, precision=FULL_PRECISION))
    activated = lowered_input(swiglu(gate_up))
    expert_out = lowered_gradient(lowered_input(jnp.einsum('ecf,efd->ecd', activated, w_down, precision=FULL_PRECISION))).reshape(EXPERTS * CAP, MODEL_DIM)
    picked = expert_out[slot_index].reshape(SEQUENCE_TOKENS, TOP, MODEL_DIM)
    combined = lax.optimization_barrier(jnp.sum(gates[:, :, None] * picked, axis=1))
    return hidden + RES_MULT * combined

def reference(tokens, positions, routes, gates, cotangent, attn_gain, w_query, key_weight, value_weight, w_out, ffn_gain, w_gate_up, w_down):
    per_group = N_SHARD
    groups = tokens.shape[0] // (SEQUENCE_TOKENS * per_group)

    def shaped(array):
        return array.reshape((groups, per_group, SEQUENCE_TOKENS) + array.shape[1:])
    fixed_inputs = (shaped(positions), shaped(routes), shaped(gates.astype(jnp.float32)))

    def forward(token_values, gain_attn, query_w, key_w, value_w, out_w, gain_ffn, inner_w, down_w):

        def one_sequence(seq_tokens, seq_positions, seq_routes, seq_gates):
            return layer(seq_tokens, seq_positions, seq_routes, seq_gates, gain_attn, query_w, key_w, value_w, out_w, gain_ffn, inner_w, down_w)

        def group_step(pieces):
            return jax.vmap(one_sequence)(pieces[0], pieces[1], pieces[2], pieces[3])
        outputs = lax.map(jax.checkpoint(group_step), (shaped(token_values),) + fixed_inputs)
        return outputs.reshape(token_values.shape)
    floats = [array.astype(jnp.float32) for array in (tokens, attn_gain, w_query, key_weight, value_weight, w_out, ffn_gain, w_gate_up, w_down)]
    output, pull_back = jax.vjp(forward, *floats)
    gradients = pull_back(cotangent.astype(jnp.float32))
    return (output.astype(jnp.bfloat16), gradients[0].astype(jnp.bfloat16), gradients[1], gradients[2], gradients[3], gradients[4], gradients[5], gradients[6], gradients[7], gradients[8])
```

```python
import jax
import jax.numpy as jnp
from jax import lax
from jax.sharding import PartitionSpec as P

QUERY_HEADS = 16
KEY_VALUE_HEADS = 8
HEAD_DIM = 64
F = 512
EXPERTS = 8
TOP = 2
CAP = 48


RMS_EPS = 1e-06
RES_MULT = 0.22
ATT_MULT = 0.015625
ROPE_BASE = 10000.0


def rms_norm(values, norm_gain):
    inverse = lax.rsqrt(jnp.mean(values * values, axis=-1, keepdims=True) + RMS_EPS)
    return values * inverse * norm_gain


def rope_tables(positions):
    half_dim = HEAD_DIM // 2
    frequency = ROPE_BASE ** (-(2.0 * jnp.arange(half_dim, dtype=jnp.float32)) / HEAD_DIM)
    angles = positions.astype(jnp.float32)[:, None] * frequency[None, :]
    return (jnp.cos(angles)[:, None, :], jnp.sin(angles)[:, None, :])


def apply_rotary(values, cosine_table, sinusoid_table):
    half_dim = values.shape[-1] // 2
    front_half = values[..., :half_dim]
    back_half = values[..., half_dim:]
    return jnp.concatenate(
        [
            front_half * cosine_table - back_half * sinusoid_table,
            back_half * cosine_table + front_half * sinusoid_table,
        ],
        axis=-1,
    )


def swiglu(gate_up):
    return jax.nn.silu(gate_up[..., :F]) * gate_up[..., F:]


def slot_table(routes):
    flat_routes = routes.reshape(-1)
    onehot = (flat_routes[:, None] == jnp.arange(EXPERTS, dtype=jnp.int32)[None, :]).astype(
        jnp.int32
    )
    before = jnp.cumsum(onehot, axis=0) - onehot
    ranked = jnp.sum(before * onehot, axis=1)
    slot_index = flat_routes * CAP + ranked
    owners = jnp.arange(flat_routes.shape[0], dtype=jnp.int32) // TOP
    sources = jnp.zeros((EXPERTS * CAP,), jnp.int32).at[slot_index].set(owners)
    filled = jnp.zeros((EXPERTS * CAP,), jnp.float32).at[slot_index].set(1.0)
    return (slot_index, sources, filled)


def masked_scores(query_head_rows, key_head_rows, causal):
    scores = ATT_MULT * jnp.einsum(
        "qhgd,khd->hgqk", query_head_rows, key_head_rows, preferred_element_type=jnp.float32
    )
    return jnp.where(causal, scores, -1e30)


def per_device(
    tokens,
    positions,
    routes,
    gates,
    cotangent,
    attn_gain,
    w_query,
    key_weight,
    value_weight,
    w_out,
    ffn_gain,
    w_gate_up,
    w_down,
):
    sequence_length = tokens.shape[0]
    model_width = tokens.shape[1]
    heads_per_group = QUERY_HEADS // KEY_VALUE_HEADS
    cosine_table, sinusoid_table = rope_tables(positions)
    causal = jnp.arange(sequence_length)[:, None] >= jnp.arange(sequence_length)[None, :]
    gain_one, full_query, full_key, full_value, full_out, gain_two = (
        lax.all_gather(attn_gain, "shard", axis=0, tiled=True),
        lax.all_gather(w_query, "shard", axis=0, tiled=True),
        lax.all_gather(key_weight, "shard", axis=0, tiled=True),
        lax.all_gather(value_weight, "shard", axis=0, tiled=True),
        lax.all_gather(w_out, "shard", axis=0, tiled=True),
        lax.all_gather(ffn_gain, "shard", axis=0, tiled=True),
    )
    inputs = tokens.astype(jnp.float32)
    normalized_input, norm_pull = jax.vjp(rms_norm, inputs, gain_one.astype(jnp.float32))
    normed_low = normalized_input.astype(jnp.bfloat16)
    query_proj = jnp.dot(normed_low, full_query, preferred_element_type=jnp.float32).reshape(
        sequence_length, QUERY_HEADS, HEAD_DIM
    )
    key_proj = jnp.dot(normed_low, full_key, preferred_element_type=jnp.float32).reshape(
        sequence_length, KEY_VALUE_HEADS, HEAD_DIM
    )
    value_head_rows = (
        jnp.dot(normed_low, full_value, preferred_element_type=jnp.float32)
        .astype(jnp.bfloat16)
        .reshape(sequence_length, KEY_VALUE_HEADS, HEAD_DIM)
    )
    query_head_rows = (
        apply_rotary(query_proj, cosine_table, sinusoid_table)
        .astype(jnp.bfloat16)
        .reshape(sequence_length, KEY_VALUE_HEADS, heads_per_group, HEAD_DIM)
    )
    key_head_rows = apply_rotary(key_proj, cosine_table, sinusoid_table).astype(jnp.bfloat16)
    scores = masked_scores(query_head_rows, key_head_rows, causal)
    top_score = jnp.max(scores, axis=-1, keepdims=True)
    log_total = top_score + jnp.log(jnp.sum(jnp.exp(scores - top_score), axis=-1, keepdims=True))
    probs_low = jnp.exp(scores - log_total).astype(jnp.bfloat16)
    attended = jnp.einsum(
        "hgqk,khd->qhgd", probs_low, value_head_rows, preferred_element_type=jnp.float32
    )
    attended = attended.reshape(sequence_length, QUERY_HEADS * HEAD_DIM).astype(jnp.bfloat16)
    branch = jnp.dot(attended, full_out, preferred_element_type=jnp.float32)
    hidden = inputs + RES_MULT * branch
    second, second_pull = jax.vjp(rms_norm, hidden, gain_two.astype(jnp.float32))
    second_low = second.astype(jnp.bfloat16)
    slot_index, sources, filled = slot_table(routes)
    dispatched = (second_low[sources] * filled[:, None].astype(jnp.bfloat16)).reshape(
        EXPERTS, CAP, model_width
    )
    received = lax.all_to_all(dispatched, "shard", split_axis=0, concat_axis=1, tiled=True)
    gate_up = jnp.einsum("ecd,edf->ecf", received, w_gate_up, preferred_element_type=jnp.float32)
    activated, act_pull = jax.vjp(swiglu, gate_up)
    act_low = activated.astype(jnp.bfloat16)
    expert_out = jnp.einsum(
        "ecf,efd->ecd", act_low, w_down, preferred_element_type=jnp.float32
    ).astype(jnp.bfloat16)
    returned = lax.all_to_all(expert_out, "shard", split_axis=1, concat_axis=0, tiled=True).reshape(
        EXPERTS * CAP, model_width
    )
    picked = returned[slot_index].reshape(sequence_length, TOP, model_width).astype(jnp.float32)
    combined = jnp.sum(gates[:, :, None] * picked, axis=1)
    output = (hidden + RES_MULT * combined).astype(jnp.bfloat16)
    upstream = cotangent.astype(jnp.float32)
    route_grad = (gates[:, :, None] * (RES_MULT * upstream)[:, None, :]).astype(jnp.bfloat16)
    route_grad = route_grad.reshape(sequence_length * TOP, model_width)
    out_grad = jnp.zeros((EXPERTS * CAP, model_width), jnp.bfloat16).at[slot_index].set(route_grad)
    out_grad = out_grad.reshape(EXPERTS, CAP, model_width)
    grad_arrived = lax.all_to_all(out_grad, "shard", split_axis=0, concat_axis=1, tiled=True)
    outbound_grad = jnp.einsum(
        "ecf,ecd->efd", act_low, grad_arrived, preferred_element_type=jnp.float32
    )
    act_grad = jnp.einsum("ecd,efd->ecf", grad_arrived, w_down, preferred_element_type=jnp.float32)
    inner_grad = act_pull(act_grad)[0].astype(jnp.bfloat16)
    inbound_grad = jnp.einsum(
        "ecd,ecf->edf", received, inner_grad, preferred_element_type=jnp.float32
    )
    rows_grad = jnp.einsum(
        "ecf,edf->ecd", inner_grad, w_gate_up, preferred_element_type=jnp.float32
    ).astype(jnp.bfloat16)
    rows_back = lax.all_to_all(rows_grad, "shard", split_axis=1, concat_axis=0, tiled=True).reshape(
        EXPERTS * CAP, model_width
    )
    second_grad = jnp.sum(
        rows_back[slot_index].reshape(sequence_length, TOP, model_width).astype(jnp.float32), axis=1
    )
    hidden_part, grad_latter = second_pull(second_grad)
    hidden_grad = upstream + hidden_part
    full_query, full_key, full_value, full_out = (
        lax.all_gather(w_query, "shard", axis=0, tiled=True),
        lax.all_gather(key_weight, "shard", axis=0, tiled=True),
        lax.all_gather(value_weight, "shard", axis=0, tiled=True),
        lax.all_gather(w_out, "shard", axis=0, tiled=True),
    )
    branch_grad = (RES_MULT * hidden_grad).astype(jnp.bfloat16)
    attended_gradient = jnp.dot(branch_grad, full_out.T, preferred_element_type=jnp.float32).astype(
        jnp.bfloat16
    )
    attended_gradient = attended_gradient.reshape(
        sequence_length, KEY_VALUE_HEADS, heads_per_group, HEAD_DIM
    )
    rescored = masked_scores(query_head_rows, key_head_rows, causal)
    probs = jnp.exp(rescored - log_total)
    probs_again = probs.astype(jnp.bfloat16)
    probs_grad = jnp.einsum(
        "qhgd,khd->hgqk", attended_gradient, value_head_rows, preferred_element_type=jnp.float32
    )
    row_inner = jnp.sum(probs * probs_grad, axis=-1, keepdims=True)
    score_grad = (probs * (probs_grad - row_inner)).astype(jnp.bfloat16)
    value_gradient = jnp.einsum(
        "hgqk,qhgd->khd", probs_again, attended_gradient, preferred_element_type=jnp.float32
    )
    value_gradient = value_gradient.astype(jnp.bfloat16).reshape(
        sequence_length, KEY_VALUE_HEADS * HEAD_DIM
    )
    query_turned = ATT_MULT * jnp.einsum(
        "hgqk,khd->qhgd", score_grad, key_head_rows, preferred_element_type=jnp.float32
    )
    rotated_keys = ATT_MULT * jnp.einsum(
        "hgqk,qhgd->khd", score_grad, query_head_rows, preferred_element_type=jnp.float32
    )
    query_grad = (
        apply_rotary(
            query_turned.reshape(sequence_length, QUERY_HEADS, HEAD_DIM),
            cosine_table,
            -sinusoid_table,
        )
        .astype(jnp.bfloat16)
        .reshape(sequence_length, QUERY_HEADS * HEAD_DIM)
    )
    key_grad = (
        apply_rotary(rotated_keys, cosine_table, -sinusoid_table)
        .astype(jnp.bfloat16)
        .reshape(sequence_length, KEY_VALUE_HEADS * HEAD_DIM)
    )
    normed_grad = jnp.dot(query_grad, full_query.T, preferred_element_type=jnp.float32)
    normed_grad = normed_grad + jnp.dot(key_grad, full_key.T, preferred_element_type=jnp.float32)
    normed_grad = normed_grad + jnp.dot(
        value_gradient, full_value.T, preferred_element_type=jnp.float32
    )
    input_part, grad_former = norm_pull(normed_grad)
    input_grad = (hidden_grad + input_part).astype(jnp.bfloat16)
    projected = jnp.concatenate([query_grad, key_grad, value_gradient], axis=1)
    proj_grad = jnp.dot(attended.T, branch_grad, preferred_element_type=jnp.float32)
    proj_owned = lax.psum_scatter(
        jnp.dot(normed_low.T, projected, preferred_element_type=jnp.float32).astype(jnp.bfloat16),
        "shard",
        scatter_dimension=0,
        tiled=True,
    ).astype(jnp.float32)
    owned_out, owned_former, owned_latter = (
        lax.psum_scatter(
            proj_grad.astype(jnp.bfloat16), "shard", scatter_dimension=0, tiled=True
        ).astype(jnp.float32),
        lax.psum_scatter(
            grad_former.astype(jnp.bfloat16), "shard", scatter_dimension=0, tiled=True
        ).astype(jnp.float32),
        lax.psum_scatter(
            grad_latter.astype(jnp.bfloat16), "shard", scatter_dimension=0, tiled=True
        ).astype(jnp.float32),
    )
    query_cols = QUERY_HEADS * HEAD_DIM
    key_columns = KEY_VALUE_HEADS * HEAD_DIM
    owned_query = proj_owned[:, :query_cols]
    owned_key = proj_owned[:, query_cols : query_cols + key_columns]
    owned_value = proj_owned[:, query_cols + key_columns :]
    (
        summed_former,
        summed_query,
        summed_key,
        summed_value,
        summed_out,
        summed_latter,
        summed_inbound,
        summed_outbound,
    ) = (
        lax.psum(owned_former.astype(jnp.bfloat16), "rep").astype(jnp.float32),
        lax.psum(owned_query.astype(jnp.bfloat16), "rep").astype(jnp.float32),
        lax.psum(owned_key.astype(jnp.bfloat16), "rep").astype(jnp.float32),
        lax.psum(owned_value.astype(jnp.bfloat16), "rep").astype(jnp.float32),
        lax.psum(owned_out.astype(jnp.bfloat16), "rep").astype(jnp.float32),
        lax.psum(owned_latter.astype(jnp.bfloat16), "rep").astype(jnp.float32),
        lax.psum(inbound_grad.astype(jnp.bfloat16), "rep").astype(jnp.float32),
        lax.psum(outbound_grad.astype(jnp.bfloat16), "rep").astype(jnp.float32),
    )
    return (
        output,
        input_grad,
        summed_former,
        summed_query,
        summed_key,
        summed_value,
        summed_out,
        summed_latter,
        summed_inbound,
        summed_outbound,
    )


PAIR = [(0, 1), (1, 0)]


def swap(values, axis):
    return lax.ppermute(values, axis, PAIR)


def bf(values):
    return values.astype(jnp.bfloat16)


def f32(values):
    return values.astype(jnp.float32)


def dot(left, right):
    return jnp.dot(left, right, preferred_element_type=jnp.float32)


def dot_nt(left, right):
    return lax.dot_general(left, right, (((1,), (1,)), ((), ())), preferred_element_type=jnp.float32)


def dot_tn(left, right):
    return lax.dot_general(left, right, (((0,), (0,)), ((), ())), preferred_element_type=jnp.float32)


def ein(spec, left, right):
    return jnp.einsum(spec, left, right, preferred_element_type=jnp.float32)


def gather_group(rows):
    half = rows.shape[1] // 2
    first, second = rows[:, :half], rows[:, half:]
    first = jnp.stack([first, swap(first, "x")])
    second = jnp.stack([second, swap(second, "y")])
    first = jnp.stack([first, swap(first, "y")])
    second = jnp.stack([second, swap(second, "x")], axis=1)
    halves = []
    for part in (first, second):
        both = jnp.stack([part, swap(part, "core")])
        halves.append(both.reshape((8,) + rows.shape[:1] + (half,)))
    return halves


def scatter_group(parts):
    half = parts.shape[-1] // 2
    kept = bf(f32(parts[0]) + f32(swap(parts[1], "core")))
    first, second = kept[..., :half], kept[..., half:]
    first = bf(f32(first[:, 0]) + f32(swap(first[:, 1], "x")))
    second = bf(f32(second[0]) + f32(swap(second[1], "y")))
    first = f32(first[0]) + f32(swap(first[1], "y"))
    second = f32(second[0]) + f32(swap(second[1], "x"))
    return jnp.concatenate([first, second], axis=1)


def per_device_split(
    tokens,
    positions,
    routes,
    gates,
    cotangent,
    attn_gain,
    w_query,
    key_weight,
    value_weight,
    w_out,
    ffn_gain,
    w_gate_up,
    w_down,
):
    length, width = tokens.shape
    half_width = width // 2
    heads = KEY_VALUE_HEADS // 2
    grouped = QUERY_HEADS // KEY_VALUE_HEADS
    q_cols = heads * grouped * HEAD_DIM
    k_cols = heads * HEAD_DIM
    here = lax.axis_index("x")
    member = lax.axis_index("y") * 2 + lax.axis_index("core")
    expert = here * 4 + member

    def mine(values, axis):
        size = values.shape[axis] // 2
        return lax.dynamic_slice_in_dim(values, here * size, size, axis)

    def other(values, axis):
        size = values.shape[axis] // 2
        return lax.dynamic_slice_in_dim(values, (1 - here) * size, size, axis)

    def ordered(own, received, axis):
        return jnp.where(
            here == 0,
            jnp.concatenate([own, received], axis),
            jnp.concatenate([received, own], axis),
        )

    def turned(values):
        return jnp.concatenate([values[length:], values[:length]], axis=0)

    inputs = f32(tokens)
    inverse = lax.rsqrt(jnp.mean(inputs * inputs, axis=-1, keepdims=True) + RMS_EPS)
    own_cols = mine(tokens, 1)
    their_cols = swap(other(tokens, 1), "x")
    facts = jnp.concatenate(
        [
            gates.T,
            f32(routes).T,
            f32(positions)[None],
            inverse.T,
            f32(ffn_gain).reshape(-1, length),
        ],
        axis=0,
    )
    facts = jnp.pad(facts, ((0, -facts.shape[0] % 8), (0, 0)))
    their_facts = swap(facts, "x")
    facts_pair = jnp.stack([facts, their_facts])
    facts_quad = jnp.stack([facts_pair, swap(facts_pair, "y")])
    facts_all = jnp.stack([facts_quad, swap(facts_quad, "core")]).reshape((8,) + facts.shape)

    gain_one = f32(attn_gain)
    normed = jnp.concatenate(
        [
            bf(f32(own_cols) * inverse * gain_one),
            bf(f32(their_cols) * their_facts[5][:, None] * gain_one),
        ],
        axis=0,
    )
    partial = [dot(normed, w) for w in (w_query, key_weight, value_weight)]
    sent = jnp.concatenate([bf(other(p, 1)) for p in partial], axis=1)
    arrived = turned(swap(sent, "x"))
    kept = jnp.concatenate([mine(p, 1) for p in partial], axis=1) + f32(arrived)
    place = jnp.stack([facts[4], their_facts[4]])
    half_dim = HEAD_DIM // 2
    frequency = ROPE_BASE ** (-(2.0 * jnp.arange(half_dim, dtype=jnp.float32)) / HEAD_DIM)
    angles = place[:, :, None] * frequency
    cosine, sinusoid = jnp.cos(angles)[:, :, None, :], jnp.sin(angles)[:, :, None, :]
    q = bf(apply_rotary(kept[:, :q_cols].reshape(2, length, -1, HEAD_DIM), cosine, sinusoid))
    k = bf(
        apply_rotary(
            kept[:, q_cols : q_cols + k_cols].reshape(2, length, -1, HEAD_DIM), cosine, sinusoid
        )
    )
    v = bf(kept[:, q_cols + k_cols :]).reshape(2, length, heads, HEAD_DIM)
    q = q.reshape(2, length, heads, grouped, HEAD_DIM)
    causal = jnp.arange(length)[:, None] >= jnp.arange(length)[None, :]
    scores = jnp.where(causal, ATT_MULT * ein("sqhgd,skhd->shgqk", q, k), -1e30)
    probs = jax.nn.softmax(scores, axis=-1)
    probs_low = bf(probs)
    attended = bf(ein("shgqk,skhd->sqhgd", probs_low, v)).reshape(2 * length, q_cols)
    branch = dot(attended, w_out)
    hidden = inputs + RES_MULT * (branch[:length] + f32(swap(bf(branch[length:]), "x")))
    gain_rows = half_width // length
    gain_two = ordered(
        facts[6 : 6 + gain_rows].reshape(-1), their_facts[6 : 6 + gain_rows].reshape(-1), 0
    )
    inverse_two = lax.rsqrt(jnp.mean(hidden * hidden, axis=-1, keepdims=True) + RMS_EPS)
    second = bf(hidden * inverse_two * gain_two)

    match = f32(facts_all[:, 2:4] == f32(expert))
    taken = jnp.sum(match, axis=1)
    gate = jnp.sum(facts_all[:, 0:2] * match, axis=1)
    rank = dot(bf(taken), bf(jnp.arange(length)[:, None] < jnp.arange(length)[None, :]))
    slots = jnp.arange(CAP, dtype=jnp.float32)
    pick = bf((rank[:, None, :] == slots[None, :, None]) & (taken[:, None, :] > 0))
    w_in = lax.dynamic_index_in_dim(w_gate_up, member, 0, keepdims=False)
    w_back = lax.dynamic_index_in_dim(w_down, member, 0, keepdims=False)

    def dispatch(values):
        return bf(ein("sct,std->scd", pick, values)).reshape(8 * CAP, -1)

    def undispatch(values):
        return ein("sct,scd->std", pick, values.reshape(8, CAP, -1))

    upstream = f32(cotangent)
    later, _ = lax.optimization_barrier((cotangent, arrived))
    out_grad = jnp.concatenate(
        [dispatch(bf(gate[:, :, None] * (RES_MULT * f32(part)))) for part in gather_group(later)],
        axis=1,
    )
    act_grad = dot_nt(out_grad, w_back)
    rows = jnp.concatenate([dispatch(part) for part in gather_group(second)], axis=1)
    gate_up = dot(rows, w_in)
    front, back = gate_up[:, :F], gate_up[:, F:]
    sigmoid = jax.nn.sigmoid(front)
    silu = front * sigmoid
    activated = bf(silu * back)
    inner = jnp.concatenate(
        [
            bf(act_grad * back * (sigmoid * (1.0 + front * (1.0 - sigmoid)))),
            bf(act_grad * silu),
        ],
        axis=1,
    )
    rows_grad = bf(dot_nt(inner, w_in))
    shape = (2, 2, 2, length, width)
    second_grad = scatter_group(bf(undispatch(rows_grad)).reshape(shape))
    grad_down = bf(dot_tn(activated, out_grad))
    grad_gate_up = bf(dot_tn(rows, inner))
    expert_out = bf(dot(activated, w_back))
    combined = scatter_group(bf(gate[:, :, None] * undispatch(expert_out)).reshape(shape))
    output = bf(hidden + RES_MULT * combined)

    cotan = second_grad * gain_two
    hidden_grad = (
        upstream
        + inverse_two * cotan
        - hidden * inverse_two**3 * jnp.mean(cotan * hidden, axis=-1, keepdims=True)
    )
    gain_grad = jnp.sum(second_grad * hidden * inverse_two, axis=0, keepdims=True)
    branch_grad = bf(RES_MULT * hidden_grad)
    both = jnp.concatenate([branch_grad, bf(jnp.pad(gain_grad, ((0, 15), (0, 0))))], axis=0)
    theirs = swap(both, "x")
    grad_ffn = mine(gain_grad + f32(theirs[length : length + 1]), 1)
    branch_pair = jnp.concatenate([branch_grad, theirs[:length]], axis=0)
    att_grad = bf(dot_nt(branch_pair, w_out)).reshape(2, length, heads, grouped, HEAD_DIM)
    grad_out = bf(dot_tn(attended, branch_pair))
    probs_grad = ein("sqhgd,skhd->shgqk", att_grad, v)
    inner_sum = jnp.sum(probs * probs_grad, axis=-1, keepdims=True)
    score_grad = bf(probs * (probs_grad - inner_sum))
    v_grad = bf(ein("shgqk,sqhgd->skhd", probs_low, att_grad)).reshape(2 * length, -1)
    q_grad = ATT_MULT * ein("shgqk,skhd->sqhgd", score_grad, k)
    k_grad = ATT_MULT * ein("shgqk,sqhgd->skhd", score_grad, q)
    q_grad = bf(apply_rotary(q_grad.reshape(2, length, -1, HEAD_DIM), cosine, -sinusoid))
    k_grad = bf(apply_rotary(k_grad, cosine, -sinusoid))
    turned_grad = jnp.concatenate(
        [q_grad.reshape(2 * length, -1), k_grad.reshape(2 * length, -1), v_grad], axis=1
    )
    their_grad = turned(swap(turned_grad, "x"))
    pieces = []
    for lo, hi in ((0, q_cols), (q_cols, q_cols + k_cols), (q_cols + k_cols, q_cols + 2 * k_cols)):
        pieces.append(ordered(turned_grad[:, lo:hi], their_grad[:, lo:hi], 1))
    normed_grad = (
        dot_nt(pieces[0], w_query) + dot_nt(pieces[1], key_weight) + dot_nt(pieces[2], value_weight)
    )
    weighted = normed_grad * gain_one
    full = ordered(weighted[:length], f32(swap(bf(weighted[length:]), "x")), 1)
    input_grad = bf(
        hidden_grad
        + inverse * full
        - inputs * inverse**3 * jnp.mean(full * inputs, axis=-1, keepdims=True)
    )
    scaled = jnp.concatenate(
        [f32(own_cols) * inverse, f32(their_cols) * their_facts[5][:, None]], axis=0
    )
    grad_attn = jnp.sum(normed_grad * scaled, axis=0, keepdims=True)
    grads = [bf(dot_tn(normed, piece)) for piece in pieces]
    return (output, input_grad, grad_attn, grad_ffn, grads, grad_out, grad_gate_up, grad_down)


def split_step(*arrays):
    output, input_grad, grad_attn, grad_ffn, grads, grad_out, grad_gate_up, grad_down = (
        per_device_split(*arrays)
    )
    def over_group(values):
        part = lax.psum_scatter(values, "z", scatter_dimension=0, tiled=True)
        whole = lax.all_gather(part, ("y", "core", "z"), axis=0, tiled=True)
        return f32(whole).reshape((4,) + values.shape)

    rows = grads[0].shape[0]
    sums = jnp.concatenate(
        [
            jnp.concatenate(list(grads) + [grad_out], axis=1),
            jnp.pad(
                bf(jnp.concatenate([grad_attn, grad_ffn], axis=0)),
                ((0, 14), (0, sum(g.shape[1] for g in grads) + grad_out.shape[1] - rows)),
            ),
        ],
        axis=0,
    )
    sum_down = over_group(grad_down)
    sum_gate_up = over_group(grad_gate_up)
    sums = f32(lax.psum(sums, ("z", "y", "core")))
    cuts, at = [], 0
    for g in list(grads) + [grad_out]:
        cuts.append(sums[:rows, at : at + g.shape[1]])
        at += g.shape[1]
    return (
        output,
        input_grad,
        sums[rows, :rows],
        cuts[0],
        cuts[1],
        cuts[2],
        cuts[3],
        sums[rows + 1, :rows],
        sum_gate_up,
        sum_down,
    )


def solution(mesh):
    replicas, shards = mesh.devices.shape
    if shards == 2 and EXPERTS == 8 and replicas % 4 == 0:
        split = jax.sharding.Mesh(
            mesh.devices.reshape(replicas // 4, 2, 2, 2), ("z", "y", "core", "x")
        )
        return mapped(split_step, split, ("z", "y", "core", "x"), "x")
    return mapped(per_device, mesh, ("rep", "shard"), "shard")


def mapped(step, mesh, every, shard):
    in_specs = (
        P(every, None),
        P(every),
        P(every, None),
        P(every, None),
        P(every, None),
        P(shard),
        P(shard, None),
        P(shard, None),
        P(shard, None),
        P(shard, None),
        P(shard),
        P(shard, None, None),
        P(shard, None, None),
    )
    out_specs = (
        P(every, None),
        P(every, None),
        P(shard),
        P(shard, None),
        P(shard, None),
        P(shard, None),
        P(shard, None),
        P(shard),
        P(shard, None, None),
        P(shard, None, None),
    )
    return jax.shard_map(step, mesh=mesh, in_specs=in_specs, out_specs=out_specs, check_vma=False)
```

```python
import jax
import jax.numpy as jnp
from jax import lax
from jax.experimental import pallas as pl
from jax.experimental.pallas import tpu as pltpu
from jax.sharding import PartitionSpec as P

QUERY_HEADS = 16
KEY_VALUE_HEADS = 8
HEAD_DIM = 64
F = 512
EXPERTS = 8
TOP = 2
CAP = 48


RMS_EPS = 1e-06
RES_MULT = 0.22
ATT_MULT = 0.015625
ROPE_BASE = 10000.0


def rms_norm(values, norm_gain):
    inverse = lax.rsqrt(jnp.mean(values * values, axis=-1, keepdims=True) + RMS_EPS)
    return values * inverse * norm_gain


def rope_tables(positions):
    half_dim = HEAD_DIM // 2
    frequency = ROPE_BASE ** (-(2.0 * jnp.arange(half_dim, dtype=jnp.float32)) / HEAD_DIM)
    angles = positions.astype(jnp.float32)[:, None] * frequency[None, :]
    return (jnp.cos(angles)[:, None, :], jnp.sin(angles)[:, None, :])


def apply_rotary(values, cosine_table, sinusoid_table):
    half_dim = values.shape[-1] // 2
    front_half = values[..., :half_dim]
    back_half = values[..., half_dim:]
    return jnp.concatenate(
        [
            front_half * cosine_table - back_half * sinusoid_table,
            back_half * cosine_table + front_half * sinusoid_table,
        ],
        axis=-1,
    )


def swiglu(gate_up):
    return jax.nn.silu(gate_up[..., :F]) * gate_up[..., F:]


def slot_table(routes):
    flat_routes = routes.reshape(-1)
    onehot = (flat_routes[:, None] == jnp.arange(EXPERTS, dtype=jnp.int32)[None, :]).astype(
        jnp.int32
    )
    before = jnp.cumsum(onehot, axis=0) - onehot
    ranked = jnp.sum(before * onehot, axis=1)
    slot_index = flat_routes * CAP + ranked
    owners = jnp.arange(flat_routes.shape[0], dtype=jnp.int32) // TOP
    sources = jnp.zeros((EXPERTS * CAP,), jnp.int32).at[slot_index].set(owners)
    filled = jnp.zeros((EXPERTS * CAP,), jnp.float32).at[slot_index].set(1.0)
    return (slot_index, sources, filled)


def masked_scores(query_head_rows, key_head_rows, causal):
    scores = ATT_MULT * jnp.einsum(
        "qhgd,khd->hgqk", query_head_rows, key_head_rows, preferred_element_type=jnp.float32
    )
    return jnp.where(causal, scores, -1e30)


def per_device(
    tokens,
    positions,
    routes,
    gates,
    cotangent,
    attn_gain,
    w_query,
    key_weight,
    value_weight,
    w_out,
    ffn_gain,
    w_gate_up,
    w_down,
):
    sequence_length = tokens.shape[0]
    model_width = tokens.shape[1]
    heads_per_group = QUERY_HEADS // KEY_VALUE_HEADS
    cosine_table, sinusoid_table = rope_tables(positions)
    causal = jnp.arange(sequence_length)[:, None] >= jnp.arange(sequence_length)[None, :]
    gain_one, full_query, full_key, full_value, full_out, gain_two = (
        lax.all_gather(attn_gain, "shard", axis=0, tiled=True),
        lax.all_gather(w_query, "shard", axis=0, tiled=True),
        lax.all_gather(key_weight, "shard", axis=0, tiled=True),
        lax.all_gather(value_weight, "shard", axis=0, tiled=True),
        lax.all_gather(w_out, "shard", axis=0, tiled=True),
        lax.all_gather(ffn_gain, "shard", axis=0, tiled=True),
    )
    inputs = tokens.astype(jnp.float32)
    normalized_input, norm_pull = jax.vjp(rms_norm, inputs, gain_one.astype(jnp.float32))
    normed_low = normalized_input.astype(jnp.bfloat16)
    query_proj = jnp.dot(normed_low, full_query, preferred_element_type=jnp.float32).reshape(
        sequence_length, QUERY_HEADS, HEAD_DIM
    )
    key_proj = jnp.dot(normed_low, full_key, preferred_element_type=jnp.float32).reshape(
        sequence_length, KEY_VALUE_HEADS, HEAD_DIM
    )
    value_head_rows = (
        jnp.dot(normed_low, full_value, preferred_element_type=jnp.float32)
        .astype(jnp.bfloat16)
        .reshape(sequence_length, KEY_VALUE_HEADS, HEAD_DIM)
    )
    query_head_rows = (
        apply_rotary(query_proj, cosine_table, sinusoid_table)
        .astype(jnp.bfloat16)
        .reshape(sequence_length, KEY_VALUE_HEADS, heads_per_group, HEAD_DIM)
    )
    key_head_rows = apply_rotary(key_proj, cosine_table, sinusoid_table).astype(jnp.bfloat16)
    scores = masked_scores(query_head_rows, key_head_rows, causal)
    top_score = jnp.max(scores, axis=-1, keepdims=True)
    log_total = top_score + jnp.log(jnp.sum(jnp.exp(scores - top_score), axis=-1, keepdims=True))
    probs_low = jnp.exp(scores - log_total).astype(jnp.bfloat16)
    attended = jnp.einsum(
        "hgqk,khd->qhgd", probs_low, value_head_rows, preferred_element_type=jnp.float32
    )
    attended = attended.reshape(sequence_length, QUERY_HEADS * HEAD_DIM).astype(jnp.bfloat16)
    branch = jnp.dot(attended, full_out, preferred_element_type=jnp.float32)
    hidden = inputs + RES_MULT * branch
    second, second_pull = jax.vjp(rms_norm, hidden, gain_two.astype(jnp.float32))
    second_low = second.astype(jnp.bfloat16)
    slot_index, sources, filled = slot_table(routes)
    dispatched = (second_low[sources] * filled[:, None].astype(jnp.bfloat16)).reshape(
        EXPERTS, CAP, model_width
    )
    received = lax.all_to_all(dispatched, "shard", split_axis=0, concat_axis=1, tiled=True)
    gate_up = jnp.einsum("ecd,edf->ecf", received, w_gate_up, preferred_element_type=jnp.float32)
    activated, act_pull = jax.vjp(swiglu, gate_up)
    act_low = activated.astype(jnp.bfloat16)
    expert_out = jnp.einsum(
        "ecf,efd->ecd", act_low, w_down, preferred_element_type=jnp.float32
    ).astype(jnp.bfloat16)
    returned = lax.all_to_all(expert_out, "shard", split_axis=1, concat_axis=0, tiled=True).reshape(
        EXPERTS * CAP, model_width
    )
    picked = returned[slot_index].reshape(sequence_length, TOP, model_width).astype(jnp.float32)
    combined = jnp.sum(gates[:, :, None] * picked, axis=1)
    output = (hidden + RES_MULT * combined).astype(jnp.bfloat16)
    upstream = cotangent.astype(jnp.float32)
    route_grad = (gates[:, :, None] * (RES_MULT * upstream)[:, None, :]).astype(jnp.bfloat16)
    route_grad = route_grad.reshape(sequence_length * TOP, model_width)
    out_grad = jnp.zeros((EXPERTS * CAP, model_width), jnp.bfloat16).at[slot_index].set(route_grad)
    out_grad = out_grad.reshape(EXPERTS, CAP, model_width)
    grad_arrived = lax.all_to_all(out_grad, "shard", split_axis=0, concat_axis=1, tiled=True)
    outbound_grad = jnp.einsum(
        "ecf,ecd->efd", act_low, grad_arrived, preferred_element_type=jnp.float32
    )
    act_grad = jnp.einsum("ecd,efd->ecf", grad_arrived, w_down, preferred_element_type=jnp.float32)
    inner_grad = act_pull(act_grad)[0].astype(jnp.bfloat16)
    inbound_grad = jnp.einsum(
        "ecd,ecf->edf", received, inner_grad, preferred_element_type=jnp.float32
    )
    rows_grad = jnp.einsum(
        "ecf,edf->ecd", inner_grad, w_gate_up, preferred_element_type=jnp.float32
    ).astype(jnp.bfloat16)
    rows_back = lax.all_to_all(rows_grad, "shard", split_axis=1, concat_axis=0, tiled=True).reshape(
        EXPERTS * CAP, model_width
    )
    second_grad = jnp.sum(
        rows_back[slot_index].reshape(sequence_length, TOP, model_width).astype(jnp.float32), axis=1
    )
    hidden_part, grad_latter = second_pull(second_grad)
    hidden_grad = upstream + hidden_part
    full_query, full_key, full_value, full_out = (
        lax.all_gather(w_query, "shard", axis=0, tiled=True),
        lax.all_gather(key_weight, "shard", axis=0, tiled=True),
        lax.all_gather(value_weight, "shard", axis=0, tiled=True),
        lax.all_gather(w_out, "shard", axis=0, tiled=True),
    )
    branch_grad = (RES_MULT * hidden_grad).astype(jnp.bfloat16)
    attended_gradient = jnp.dot(branch_grad, full_out.T, preferred_element_type=jnp.float32).astype(
        jnp.bfloat16
    )
    attended_gradient = attended_gradient.reshape(
        sequence_length, KEY_VALUE_HEADS, heads_per_group, HEAD_DIM
    )
    rescored = masked_scores(query_head_rows, key_head_rows, causal)
    probs = jnp.exp(rescored - log_total)
    probs_again = probs.astype(jnp.bfloat16)
    probs_grad = jnp.einsum(
        "qhgd,khd->hgqk", attended_gradient, value_head_rows, preferred_element_type=jnp.float32
    )
    row_inner = jnp.sum(probs * probs_grad, axis=-1, keepdims=True)
    score_grad = (probs * (probs_grad - row_inner)).astype(jnp.bfloat16)
    value_gradient = jnp.einsum(
        "hgqk,qhgd->khd", probs_again, attended_gradient, preferred_element_type=jnp.float32
    )
    value_gradient = value_gradient.astype(jnp.bfloat16).reshape(
        sequence_length, KEY_VALUE_HEADS * HEAD_DIM
    )
    query_turned = ATT_MULT * jnp.einsum(
        "hgqk,khd->qhgd", score_grad, key_head_rows, preferred_element_type=jnp.float32
    )
    rotated_keys = ATT_MULT * jnp.einsum(
        "hgqk,qhgd->khd", score_grad, query_head_rows, preferred_element_type=jnp.float32
    )
    query_grad = (
        apply_rotary(
            query_turned.reshape(sequence_length, QUERY_HEADS, HEAD_DIM),
            cosine_table,
            -sinusoid_table,
        )
        .astype(jnp.bfloat16)
        .reshape(sequence_length, QUERY_HEADS * HEAD_DIM)
    )
    key_grad = (
        apply_rotary(rotated_keys, cosine_table, -sinusoid_table)
        .astype(jnp.bfloat16)
        .reshape(sequence_length, KEY_VALUE_HEADS * HEAD_DIM)
    )
    normed_grad = jnp.dot(query_grad, full_query.T, preferred_element_type=jnp.float32)
    normed_grad = normed_grad + jnp.dot(key_grad, full_key.T, preferred_element_type=jnp.float32)
    normed_grad = normed_grad + jnp.dot(
        value_gradient, full_value.T, preferred_element_type=jnp.float32
    )
    input_part, grad_former = norm_pull(normed_grad)
    input_grad = (hidden_grad + input_part).astype(jnp.bfloat16)
    projected = jnp.concatenate([query_grad, key_grad, value_gradient], axis=1)
    proj_grad = jnp.dot(attended.T, branch_grad, preferred_element_type=jnp.float32)
    proj_owned = lax.psum_scatter(
        jnp.dot(normed_low.T, projected, preferred_element_type=jnp.float32).astype(jnp.bfloat16),
        "shard",
        scatter_dimension=0,
        tiled=True,
    ).astype(jnp.float32)
    owned_out, owned_former, owned_latter = (
        lax.psum_scatter(
            proj_grad.astype(jnp.bfloat16), "shard", scatter_dimension=0, tiled=True
        ).astype(jnp.float32),
        lax.psum_scatter(
            grad_former.astype(jnp.bfloat16), "shard", scatter_dimension=0, tiled=True
        ).astype(jnp.float32),
        lax.psum_scatter(
            grad_latter.astype(jnp.bfloat16), "shard", scatter_dimension=0, tiled=True
        ).astype(jnp.float32),
    )
    query_cols = QUERY_HEADS * HEAD_DIM
    key_columns = KEY_VALUE_HEADS * HEAD_DIM
    owned_query = proj_owned[:, :query_cols]
    owned_key = proj_owned[:, query_cols : query_cols + key_columns]
    owned_value = proj_owned[:, query_cols + key_columns :]
    (
        summed_former,
        summed_query,
        summed_key,
        summed_value,
        summed_out,
        summed_latter,
        summed_inbound,
        summed_outbound,
    ) = (
        lax.psum(owned_former.astype(jnp.bfloat16), "rep").astype(jnp.float32),
        lax.psum(owned_query.astype(jnp.bfloat16), "rep").astype(jnp.float32),
        lax.psum(owned_key.astype(jnp.bfloat16), "rep").astype(jnp.float32),
        lax.psum(owned_value.astype(jnp.bfloat16), "rep").astype(jnp.float32),
        lax.psum(owned_out.astype(jnp.bfloat16), "rep").astype(jnp.float32),
        lax.psum(owned_latter.astype(jnp.bfloat16), "rep").astype(jnp.float32),
        lax.psum(inbound_grad.astype(jnp.bfloat16), "rep").astype(jnp.float32),
        lax.psum(outbound_grad.astype(jnp.bfloat16), "rep").astype(jnp.float32),
    )
    return (
        output,
        input_grad,
        summed_former,
        summed_query,
        summed_key,
        summed_value,
        summed_out,
        summed_latter,
        summed_inbound,
        summed_outbound,
    )


PAIR = [(0, 1), (1, 0)]


def swap(values, axis):
    return lax.ppermute(values, axis, PAIR)


def bf(values):
    return values.astype(jnp.bfloat16)


def f32(values):
    return values.astype(jnp.float32)


def dot(left, right):
    return jnp.dot(left, right, preferred_element_type=jnp.float32)


def dot_nt(left, right):
    return lax.dot_general(left, right, (((1,), (1,)), ((), ())), preferred_element_type=jnp.float32)


def dot_tn(left, right):
    return lax.dot_general(left, right, (((0,), (0,)), ((), ())), preferred_element_type=jnp.float32)


def ein(spec, left, right):
    return jnp.einsum(spec, left, right, preferred_element_type=jnp.float32)


def gather_group(rows):
    half = rows.shape[1] // 2
    first, second = rows[:, :half], rows[:, half:]
    first = jnp.stack([first, swap(first, "x")])
    second = jnp.stack([second, swap(second, "y")])
    first = jnp.stack([first, swap(first, "y")])
    second = jnp.stack([second, swap(second, "x")], axis=1)
    halves = []
    for part in (first, second):
        both = jnp.stack([part, swap(part, "core")])
        halves.append(both.reshape((8,) + rows.shape[:1] + (half,)))
    return halves


def scatter_group(parts):
    half = parts.shape[-1] // 2
    kept = bf(f32(parts[0]) + f32(swap(parts[1], "core")))
    first, second = kept[..., :half], kept[..., half:]
    first = bf(f32(first[:, 0]) + f32(swap(first[:, 1], "x")))
    second = bf(f32(second[0]) + f32(swap(second[1], "y")))
    first = f32(first[0]) + f32(swap(first[1], "y"))
    second = f32(second[0]) + f32(swap(second[1], "x"))
    return jnp.concatenate([first, second], axis=1)


def scatter_group_by_tokens(parts):
    half = parts.shape[-2] // 2
    first, second = parts[..., :half, :], parts[..., half:, :]
    first = bf(f32(first[0]) + f32(swap(first[1], "core")))
    second = bf(f32(second[0]) + f32(swap(second[1], "core")))
    first = bf(f32(first[:, 0]) + f32(swap(first[:, 1], "x")))
    second = bf(f32(second[0]) + f32(swap(second[1], "y")))
    first = f32(first[0]) + f32(swap(first[1], "y"))
    second = f32(second[0]) + f32(swap(second[1], "x"))
    return jnp.concatenate([first, second], axis=0)


def per_device_split(
    tokens,
    positions,
    routes,
    gates,
    cotangent,
    attn_gain,
    w_query,
    key_weight,
    value_weight,
    w_out,
    ffn_gain,
    w_gate_up,
    w_down,
):
    length, width = tokens.shape
    half_width = width // 2
    heads = KEY_VALUE_HEADS // 2
    grouped = QUERY_HEADS // KEY_VALUE_HEADS
    q_cols = heads * grouped * HEAD_DIM
    k_cols = heads * HEAD_DIM
    here = lax.axis_index("x")
    member = lax.axis_index("y") * 2 + lax.axis_index("core")
    expert = here * 4 + member

    def mine(values, axis):
        size = values.shape[axis] // 2
        return lax.dynamic_slice_in_dim(values, here * size, size, axis)

    def other(values, axis):
        size = values.shape[axis] // 2
        return lax.dynamic_slice_in_dim(values, (1 - here) * size, size, axis)

    def ordered(own, received, axis):
        return jnp.where(
            here == 0,
            jnp.concatenate([own, received], axis),
            jnp.concatenate([received, own], axis),
        )

    def turned(values):
        return jnp.concatenate([values[length:], values[:length]], axis=0)

    inputs = f32(tokens)
    inverse = lax.rsqrt(jnp.mean(inputs * inputs, axis=-1, keepdims=True) + RMS_EPS)
    own_cols = mine(tokens, 1)
    their_cols = swap(other(tokens, 1), "x")
    facts = jnp.concatenate(
        [
            gates.T,
            f32(routes).T,
            f32(positions)[None],
            inverse.T,
            f32(ffn_gain).reshape(-1, length),
        ],
        axis=0,
    )
    facts = jnp.pad(facts, ((0, -facts.shape[0] % 8), (0, 0)))
    their_facts = swap(facts, "x")
    facts_pair = jnp.stack([facts, their_facts])
    facts_quad = jnp.stack([facts_pair, swap(facts_pair, "y")])
    facts_all = jnp.stack([facts_quad, swap(facts_quad, "core")]).reshape((8,) + facts.shape)

    gain_one = f32(attn_gain)
    normed = jnp.concatenate(
        [
            bf(f32(own_cols) * inverse * gain_one),
            bf(f32(their_cols) * their_facts[5][:, None] * gain_one),
        ],
        axis=0,
    )
    partial = [dot(normed, w) for w in (w_query, key_weight, value_weight)]
    leaving = jnp.concatenate([bf(other(p, 1)) for p in partial], axis=1)
    arrived = turned(swap(leaving, "x"))
    kept = jnp.concatenate([mine(p, 1) for p in partial], axis=1) + f32(arrived)
    place = jnp.stack([facts[4], their_facts[4]])
    half_dim = HEAD_DIM // 2
    frequency = ROPE_BASE ** (-(2.0 * jnp.arange(half_dim, dtype=jnp.float32)) / HEAD_DIM)
    angles = place[:, :, None] * frequency
    cosine, sinusoid = jnp.cos(angles)[:, :, None, :], jnp.sin(angles)[:, :, None, :]
    q = bf(apply_rotary(kept[:, :q_cols].reshape(2, length, -1, HEAD_DIM), cosine, sinusoid))
    k = bf(
        apply_rotary(
            kept[:, q_cols : q_cols + k_cols].reshape(2, length, -1, HEAD_DIM), cosine, sinusoid
        )
    )
    v = bf(kept[:, q_cols + k_cols :]).reshape(2, length, heads, HEAD_DIM)
    q = q.reshape(2, length, heads, grouped, HEAD_DIM)
    causal = jnp.arange(length)[:, None] >= jnp.arange(length)[None, :]
    scores = jnp.where(causal, ATT_MULT * ein("sqhgd,skhd->shgqk", q, k), -1e30)
    probs = jax.nn.softmax(scores, axis=-1)
    probs_low = bf(probs)
    attended = bf(ein("shgqk,skhd->sqhgd", probs_low, v)).reshape(2 * length, q_cols)
    branch = dot(attended, w_out)
    hidden = inputs + RES_MULT * (branch[:length] + f32(swap(bf(branch[length:]), "x")))
    gain_rows = half_width // length
    gain_two = ordered(
        facts[6 : 6 + gain_rows].reshape(-1), their_facts[6 : 6 + gain_rows].reshape(-1), 0
    )
    inverse_two = lax.rsqrt(jnp.mean(hidden * hidden, axis=-1, keepdims=True) + RMS_EPS)
    second = bf(hidden * inverse_two * gain_two)

    match = f32(facts_all[:, 2:4] == f32(expert))
    taken = jnp.sum(match, axis=1)
    gate = jnp.sum(facts_all[:, 0:2] * match, axis=1)
    rank = dot(bf(taken), bf(jnp.arange(length)[:, None] < jnp.arange(length)[None, :]))
    slots = jnp.arange(CAP, dtype=jnp.float32)
    pick = bf((rank[:, None, :] == slots[None, :, None]) & (taken[:, None, :] > 0))
    w_in = lax.dynamic_index_in_dim(w_gate_up, member, 0, keepdims=False)
    w_back = lax.dynamic_index_in_dim(w_down, member, 0, keepdims=False)

    def dispatch(values):
        return bf(ein("sct,std->scd", pick, values)).reshape(8 * CAP, -1)

    def undispatch(values):
        return ein("sct,scd->std", pick, values.reshape(8, CAP, -1))

    upstream = f32(cotangent)
    out_grad = jnp.concatenate(
        [dispatch(bf(gate[:, :, None] * (RES_MULT * f32(part)))) for part in gather_group(cotangent)],
        axis=1,
    )
    act_grad = dot_nt(out_grad, w_back)
    rows = jnp.concatenate([dispatch(part) for part in gather_group(second)], axis=1)
    gate_up = dot(rows, w_in)
    front, back = gate_up[:, :F], gate_up[:, F:]
    sigmoid = jax.nn.sigmoid(front)
    silu = front * sigmoid
    activated = bf(silu * back)
    inner = jnp.concatenate(
        [
            bf(act_grad * back * (sigmoid * (1.0 + front * (1.0 - sigmoid)))),
            bf(act_grad * silu),
        ],
        axis=1,
    )
    rows_grad = bf(dot_nt(inner, w_in))
    shape = (2, 2, 2, length, width)
    second_grad = scatter_group(bf(undispatch(rows_grad)).reshape(shape))
    grad_down = bf(dot_tn(activated, out_grad))
    grad_gate_up = bf(dot_tn(rows, inner))
    expert_out = bf(dot(activated, w_back))
    combined = scatter_group_by_tokens(bf(gate[:, :, None] * undispatch(expert_out)).reshape(shape))

    cotan = second_grad * gain_two
    hidden_grad = (
        upstream
        + inverse_two * cotan
        - hidden * inverse_two**3 * jnp.mean(cotan * hidden, axis=-1, keepdims=True)
    )
    gain_grad = jnp.sum(second_grad * hidden * inverse_two, axis=0, keepdims=True)
    branch_grad = bf(RES_MULT * hidden_grad)
    both = jnp.concatenate([branch_grad, bf(jnp.pad(gain_grad, ((0, 15), (0, 0))))], axis=0)
    theirs = swap(both, "x")
    held, _ = lax.optimization_barrier((hidden, theirs))
    output = bf(held + RES_MULT * combined)
    grad_ffn = mine(gain_grad + f32(theirs[length : length + 1]), 1)
    branch_pair = jnp.concatenate([branch_grad, theirs[:length]], axis=0)
    att_grad = bf(dot_nt(branch_pair, w_out)).reshape(2, length, heads, grouped, HEAD_DIM)
    grad_out = bf(dot_tn(attended, branch_pair))
    probs_grad = ein("sqhgd,skhd->shgqk", att_grad, v)
    inner_sum = jnp.sum(probs * probs_grad, axis=-1, keepdims=True)
    score_grad = bf(probs * (probs_grad - inner_sum))
    v_grad = bf(ein("shgqk,sqhgd->skhd", probs_low, att_grad)).reshape(2 * length, -1)
    q_grad = ATT_MULT * ein("shgqk,skhd->sqhgd", score_grad, k)
    k_grad = ATT_MULT * ein("shgqk,sqhgd->skhd", score_grad, q)
    q_grad = bf(apply_rotary(q_grad.reshape(2, length, -1, HEAD_DIM), cosine, -sinusoid))
    k_grad = bf(apply_rotary(k_grad, cosine, -sinusoid))
    turned_grad = jnp.concatenate(
        [q_grad.reshape(2 * length, -1), k_grad.reshape(2 * length, -1), v_grad], axis=1
    )
    their_grad = turned(swap(turned_grad, "x"))
    pieces = []
    for lo, hi in ((0, q_cols), (q_cols, q_cols + k_cols), (q_cols + k_cols, q_cols + 2 * k_cols)):
        pieces.append(ordered(turned_grad[:, lo:hi], their_grad[:, lo:hi], 1))
    normed_grad = (
        dot_nt(pieces[0], w_query) + dot_nt(pieces[1], key_weight) + dot_nt(pieces[2], value_weight)
    )
    weighted = normed_grad * gain_one
    full = ordered(weighted[:length], f32(swap(bf(weighted[length:]), "x")), 1)
    input_grad = bf(
        hidden_grad
        + inverse * full
        - inputs * inverse**3 * jnp.mean(full * inputs, axis=-1, keepdims=True)
    )
    scaled = jnp.concatenate(
        [f32(own_cols) * inverse, f32(their_cols) * their_facts[5][:, None]], axis=0
    )
    grad_attn = jnp.sum(normed_grad * scaled, axis=0, keepdims=True)
    grads = [bf(dot_tn(normed, piece)) for piece in pieces]
    return (output, input_grad, grad_attn, grad_ffn, grads, grad_out, grad_gate_up, grad_down)


def over_z(part):
    chips = lax.axis_size("z")
    if chips != 4:
        return lax.psum(part, "z")
    inner = (lax.axis_index("z") + 1) // 2 == 1
    held = bf(f32(part) + f32(lax.ppermute(part, "z", [(0, 1), (3, 2)])))
    total = bf(f32(held) + f32(lax.ppermute(held, "z", [(1, 2), (2, 1)])))
    return jnp.where(inner, total, lax.ppermute(total, "z", [(1, 0), (2, 3)]))


def copies(part):
    across = swap(part, "y")
    return [part, swap(part, "core"), across, swap(across, "core")]


def quarter(values):
    for axis in ("core", "y"):
        rows = values.shape[0] // 2
        at = lax.axis_index(axis)
        own = lax.dynamic_slice_in_dim(values, at * rows, rows, 0)
        out = lax.dynamic_slice_in_dim(values, (1 - at) * rows, rows, 0)
        values = bf(f32(own) + f32(swap(out, axis)))
    return values


PIECE = 256


def put_piece(places, parts, whole, rows, block):
    size, width = parts[0].shape
    step = size // 4

    def kernel(places_ref, *refs):
        for flip in range(4):
            refs[-1][places_ref[flip]] = refs[flip][...].astype(jnp.float32)

    part_spec = pl.BlockSpec((step, width), lambda at, places: (at, 0))
    more = [] if whole is None else [whole]
    return pl.pallas_call(
        kernel,
        out_shape=jax.ShapeDtypeStruct((4, rows, width), jnp.float32),
        grid_spec=pltpu.PrefetchScalarGridSpec(
            num_scalar_prefetch=1,
            grid=(4,),
            in_specs=[part_spec] * 4 + [pl.BlockSpec(memory_space=pl.ANY)] * len(more),
            out_specs=pl.BlockSpec(
                (4, step, width), lambda at, places: (0, block * 4 + at, 0)
            ),
        ),
        input_output_aliases={5: 0} if more else {},
    )(places, *parts, *more)


def put_rows(places, parts, widths):
    size, width = parts[0].shape
    step = size // 4

    def kernel(places_ref, *refs):
        for flip in range(4):
            at = 0
            for out, cut in zip(refs[4:], widths):
                out[places_ref[flip]] = refs[flip][:, at : at + cut].astype(jnp.float32)
                at += cut

    outs = pl.pallas_call(
        kernel,
        out_shape=[jax.ShapeDtypeStruct((4, size, cut), jnp.float32) for cut in widths],
        grid_spec=pltpu.PrefetchScalarGridSpec(
            num_scalar_prefetch=1,
            grid=(4,),
            in_specs=[pl.BlockSpec((step, width), lambda at, places: (at, 0))] * 4,
            out_specs=[
                pl.BlockSpec((4, step, cut), lambda at, places: (0, at, 0)) for cut in widths
            ],
        ),
    )(places, *parts)
    return [out.reshape(4 * size, cut) for out, cut in zip(outs, widths)]


def reduced_step(*arrays):
    output, input_grad, grad_attn, grad_ffn, grads, grad_out, grad_gate_up, grad_down = (
        per_device_split(*arrays)
    )
    core, row = lax.axis_index("core"), lax.axis_index("y")
    flips = jnp.arange(4, dtype=jnp.int32)
    experts = (row * 2 + core) ^ flips
    quarters = (core ^ (flips & 1)) * 2 + (row ^ (flips >> 1))
    sums = []
    for values in (grad_down, grad_gate_up):
        whole = None
        for at in range(0, values.shape[0], PIECE):
            total = over_z(values[at : at + PIECE])
            parts = copies(total)
            rows, block = values.shape[0], at // PIECE
            whole = put_piece(experts, parts, whole, rows, block)
        sums.append(whole)
    sum_down, sum_gate_up = sums

    def over_all(pieces):
        wide = jnp.concatenate(pieces, axis=1)
        parts = copies(over_z(quarter(wide)))
        return put_rows(quarters, parts, [p.shape[1] for p in pieces])

    gains = bf(jnp.concatenate([grad_attn, grad_ffn], axis=0)).T
    (sum_out,) = over_all([grad_out])
    *sum_proj, sum_gains = over_all(grads + [jnp.pad(gains, ((0, 0), (0, 126)))])
    return (
        output,
        input_grad,
        sum_gains[:, 0],
        *sum_proj,
        sum_out,
        sum_gains[:, 1],
        sum_gate_up,
        sum_down,
    )


def solution(mesh):
    replicas, shards = mesh.devices.shape
    if shards == 2 and EXPERTS == 8 and replicas % 4 == 0:
        split = jax.sharding.Mesh(
            mesh.devices.reshape(replicas // 4, 2, 2, 2), ("z", "y", "core", "x")
        )
        step = mapped(reduced_step, split, ("z", "y", "core", "x"), "x")
        return step
    return mapped(per_device, mesh, ("rep", "shard"), "shard")


def mapped(step, mesh, every, shard):
    in_specs = (
        P(every, None),
        P(every),
        P(every, None),
        P(every, None),
        P(every, None),
        P(shard),
        P(shard, None),
        P(shard, None),
        P(shard, None),
        P(shard, None),
        P(shard),
        P(shard, None, None),
        P(shard, None, None),
    )
    out_specs = (
        P(every, None),
        P(every, None),
        P(shard),
        P(shard, None),
        P(shard, None),
        P(shard, None),
        P(shard, None),
        P(shard),
        P(shard, None, None),
        P(shard, None, None),
    )
    return jax.shard_map(step, mesh=mesh, in_specs=in_specs, out_specs=out_specs, check_vma=False)
```

```python
import jax
import jax.numpy as jnp
from jax import lax
from jax.experimental import pallas as pl
from jax.experimental.pallas import tpu as pltpu
from jax.sharding import PartitionSpec as P

QUERY_HEADS = 16
KEY_VALUE_HEADS = 8
HEAD_DIM = 64
F = 512
EXPERTS = 8
TOP = 2
CAP = 48


RMS_EPS = 1e-06
RES_MULT = 0.22
ATT_MULT = 0.015625
ROPE_BASE = 10000.0


def rms_norm(values, norm_gain):
    inverse = lax.rsqrt(jnp.mean(values * values, axis=-1, keepdims=True) + RMS_EPS)
    return values * inverse * norm_gain


def rope_tables(positions):
    half_dim = HEAD_DIM // 2
    frequency = ROPE_BASE ** (-(2.0 * jnp.arange(half_dim, dtype=jnp.float32)) / HEAD_DIM)
    angles = positions.astype(jnp.float32)[:, None] * frequency[None, :]
    return (jnp.cos(angles)[:, None, :], jnp.sin(angles)[:, None, :])


def apply_rotary(values, cosine_table, sinusoid_table):
    half_dim = values.shape[-1] // 2
    front_half = values[..., :half_dim]
    back_half = values[..., half_dim:]
    return jnp.concatenate(
        [
            front_half * cosine_table - back_half * sinusoid_table,
            back_half * cosine_table + front_half * sinusoid_table,
        ],
        axis=-1,
    )


def swiglu(gate_up):
    return jax.nn.silu(gate_up[..., :F]) * gate_up[..., F:]


def slot_table(routes):
    flat_routes = routes.reshape(-1)
    onehot = (flat_routes[:, None] == jnp.arange(EXPERTS, dtype=jnp.int32)[None, :]).astype(
        jnp.int32
    )
    before = jnp.cumsum(onehot, axis=0) - onehot
    ranked = jnp.sum(before * onehot, axis=1)
    slot_index = flat_routes * CAP + ranked
    owners = jnp.arange(flat_routes.shape[0], dtype=jnp.int32) // TOP
    sources = jnp.zeros((EXPERTS * CAP,), jnp.int32).at[slot_index].set(owners)
    filled = jnp.zeros((EXPERTS * CAP,), jnp.float32).at[slot_index].set(1.0)
    return (slot_index, sources, filled)


def masked_scores(query_head_rows, key_head_rows, causal):
    scores = ATT_MULT * jnp.einsum(
        "qhgd,khd->hgqk", query_head_rows, key_head_rows, preferred_element_type=jnp.float32
    )
    return jnp.where(causal, scores, -1e30)


def per_device(
    tokens,
    positions,
    routes,
    gates,
    cotangent,
    attn_gain,
    w_query,
    key_weight,
    value_weight,
    w_out,
    ffn_gain,
    w_gate_up,
    w_down,
):
    sequence_length = tokens.shape[0]
    model_width = tokens.shape[1]
    heads_per_group = QUERY_HEADS // KEY_VALUE_HEADS
    cosine_table, sinusoid_table = rope_tables(positions)
    causal = jnp.arange(sequence_length)[:, None] >= jnp.arange(sequence_length)[None, :]
    gain_one, full_query, full_key, full_value, full_out, gain_two = (
        lax.all_gather(attn_gain, "shard", axis=0, tiled=True),
        lax.all_gather(w_query, "shard", axis=0, tiled=True),
        lax.all_gather(key_weight, "shard", axis=0, tiled=True),
        lax.all_gather(value_weight, "shard", axis=0, tiled=True),
        lax.all_gather(w_out, "shard", axis=0, tiled=True),
        lax.all_gather(ffn_gain, "shard", axis=0, tiled=True),
    )
    inputs = tokens.astype(jnp.float32)
    normalized_input, norm_pull = jax.vjp(rms_norm, inputs, gain_one.astype(jnp.float32))
    normed_low = normalized_input.astype(jnp.bfloat16)
    query_proj = jnp.dot(normed_low, full_query, preferred_element_type=jnp.float32).reshape(
        sequence_length, QUERY_HEADS, HEAD_DIM
    )
    key_proj = jnp.dot(normed_low, full_key, preferred_element_type=jnp.float32).reshape(
        sequence_length, KEY_VALUE_HEADS, HEAD_DIM
    )
    value_head_rows = (
        jnp.dot(normed_low, full_value, preferred_element_type=jnp.float32)
        .astype(jnp.bfloat16)
        .reshape(sequence_length, KEY_VALUE_HEADS, HEAD_DIM)
    )
    query_head_rows = (
        apply_rotary(query_proj, cosine_table, sinusoid_table)
        .astype(jnp.bfloat16)
        .reshape(sequence_length, KEY_VALUE_HEADS, heads_per_group, HEAD_DIM)
    )
    key_head_rows = apply_rotary(key_proj, cosine_table, sinusoid_table).astype(jnp.bfloat16)
    scores = masked_scores(query_head_rows, key_head_rows, causal)
    top_score = jnp.max(scores, axis=-1, keepdims=True)
    log_total = top_score + jnp.log(jnp.sum(jnp.exp(scores - top_score), axis=-1, keepdims=True))
    probs_low = jnp.exp(scores - log_total).astype(jnp.bfloat16)
    attended = jnp.einsum(
        "hgqk,khd->qhgd", probs_low, value_head_rows, preferred_element_type=jnp.float32
    )
    attended = attended.reshape(sequence_length, QUERY_HEADS * HEAD_DIM).astype(jnp.bfloat16)
    branch = jnp.dot(attended, full_out, preferred_element_type=jnp.float32)
    hidden = inputs + RES_MULT * branch
    second, second_pull = jax.vjp(rms_norm, hidden, gain_two.astype(jnp.float32))
    second_low = second.astype(jnp.bfloat16)
    slot_index, sources, filled = slot_table(routes)
    dispatched = (second_low[sources] * filled[:, None].astype(jnp.bfloat16)).reshape(
        EXPERTS, CAP, model_width
    )
    received = lax.all_to_all(dispatched, "shard", split_axis=0, concat_axis=1, tiled=True)
    gate_up = jnp.einsum("ecd,edf->ecf", received, w_gate_up, preferred_element_type=jnp.float32)
    activated, act_pull = jax.vjp(swiglu, gate_up)
    act_low = activated.astype(jnp.bfloat16)
    expert_out = jnp.einsum(
        "ecf,efd->ecd", act_low, w_down, preferred_element_type=jnp.float32
    ).astype(jnp.bfloat16)
    returned = lax.all_to_all(expert_out, "shard", split_axis=1, concat_axis=0, tiled=True).reshape(
        EXPERTS * CAP, model_width
    )
    picked = returned[slot_index].reshape(sequence_length, TOP, model_width).astype(jnp.float32)
    combined = jnp.sum(gates[:, :, None] * picked, axis=1)
    output = (hidden + RES_MULT * combined).astype(jnp.bfloat16)
    upstream = cotangent.astype(jnp.float32)
    route_grad = (gates[:, :, None] * (RES_MULT * upstream)[:, None, :]).astype(jnp.bfloat16)
    route_grad = route_grad.reshape(sequence_length * TOP, model_width)
    out_grad = jnp.zeros((EXPERTS * CAP, model_width), jnp.bfloat16).at[slot_index].set(route_grad)
    out_grad = out_grad.reshape(EXPERTS, CAP, model_width)
    grad_arrived = lax.all_to_all(out_grad, "shard", split_axis=0, concat_axis=1, tiled=True)
    outbound_grad = jnp.einsum(
        "ecf,ecd->efd", act_low, grad_arrived, preferred_element_type=jnp.float32
    )
    act_grad = jnp.einsum("ecd,efd->ecf", grad_arrived, w_down, preferred_element_type=jnp.float32)
    inner_grad = act_pull(act_grad)[0].astype(jnp.bfloat16)
    inbound_grad = jnp.einsum(
        "ecd,ecf->edf", received, inner_grad, preferred_element_type=jnp.float32
    )
    rows_grad = jnp.einsum(
        "ecf,edf->ecd", inner_grad, w_gate_up, preferred_element_type=jnp.float32
    ).astype(jnp.bfloat16)
    rows_back = lax.all_to_all(rows_grad, "shard", split_axis=1, concat_axis=0, tiled=True).reshape(
        EXPERTS * CAP, model_width
    )
    second_grad = jnp.sum(
        rows_back[slot_index].reshape(sequence_length, TOP, model_width).astype(jnp.float32), axis=1
    )
    hidden_part, grad_latter = second_pull(second_grad)
    hidden_grad = upstream + hidden_part
    full_query, full_key, full_value, full_out = (
        lax.all_gather(w_query, "shard", axis=0, tiled=True),
        lax.all_gather(key_weight, "shard", axis=0, tiled=True),
        lax.all_gather(value_weight, "shard", axis=0, tiled=True),
        lax.all_gather(w_out, "shard", axis=0, tiled=True),
    )
    branch_grad = (RES_MULT * hidden_grad).astype(jnp.bfloat16)
    attended_gradient = jnp.dot(branch_grad, full_out.T, preferred_element_type=jnp.float32).astype(
        jnp.bfloat16
    )
    attended_gradient = attended_gradient.reshape(
        sequence_length, KEY_VALUE_HEADS, heads_per_group, HEAD_DIM
    )
    rescored = masked_scores(query_head_rows, key_head_rows, causal)
    probs = jnp.exp(rescored - log_total)
    probs_again = probs.astype(jnp.bfloat16)
    probs_grad = jnp.einsum(
        "qhgd,khd->hgqk", attended_gradient, value_head_rows, preferred_element_type=jnp.float32
    )
    row_inner = jnp.sum(probs * probs_grad, axis=-1, keepdims=True)
    score_grad = (probs * (probs_grad - row_inner)).astype(jnp.bfloat16)
    value_gradient = jnp.einsum(
        "hgqk,qhgd->khd", probs_again, attended_gradient, preferred_element_type=jnp.float32
    )
    value_gradient = value_gradient.astype(jnp.bfloat16).reshape(
        sequence_length, KEY_VALUE_HEADS * HEAD_DIM
    )
    query_turned = ATT_MULT * jnp.einsum(
        "hgqk,khd->qhgd", score_grad, key_head_rows, preferred_element_type=jnp.float32
    )
    rotated_keys = ATT_MULT * jnp.einsum(
        "hgqk,qhgd->khd", score_grad, query_head_rows, preferred_element_type=jnp.float32
    )
    query_grad = (
        apply_rotary(
            query_turned.reshape(sequence_length, QUERY_HEADS, HEAD_DIM),
            cosine_table,
            -sinusoid_table,
        )
        .astype(jnp.bfloat16)
        .reshape(sequence_length, QUERY_HEADS * HEAD_DIM)
    )
    key_grad = (
        apply_rotary(rotated_keys, cosine_table, -sinusoid_table)
        .astype(jnp.bfloat16)
        .reshape(sequence_length, KEY_VALUE_HEADS * HEAD_DIM)
    )
    normed_grad = jnp.dot(query_grad, full_query.T, preferred_element_type=jnp.float32)
    normed_grad = normed_grad + jnp.dot(key_grad, full_key.T, preferred_element_type=jnp.float32)
    normed_grad = normed_grad + jnp.dot(
        value_gradient, full_value.T, preferred_element_type=jnp.float32
    )
    input_part, grad_former = norm_pull(normed_grad)
    input_grad = (hidden_grad + input_part).astype(jnp.bfloat16)
    projected = jnp.concatenate([query_grad, key_grad, value_gradient], axis=1)
    proj_grad = jnp.dot(attended.T, branch_grad, preferred_element_type=jnp.float32)
    proj_owned = lax.psum_scatter(
        jnp.dot(normed_low.T, projected, preferred_element_type=jnp.float32).astype(jnp.bfloat16),
        "shard",
        scatter_dimension=0,
        tiled=True,
    ).astype(jnp.float32)
    owned_out, owned_former, owned_latter = (
        lax.psum_scatter(
            proj_grad.astype(jnp.bfloat16), "shard", scatter_dimension=0, tiled=True
        ).astype(jnp.float32),
        lax.psum_scatter(
            grad_former.astype(jnp.bfloat16), "shard", scatter_dimension=0, tiled=True
        ).astype(jnp.float32),
        lax.psum_scatter(
            grad_latter.astype(jnp.bfloat16), "shard", scatter_dimension=0, tiled=True
        ).astype(jnp.float32),
    )
    query_cols = QUERY_HEADS * HEAD_DIM
    key_columns = KEY_VALUE_HEADS * HEAD_DIM
    owned_query = proj_owned[:, :query_cols]
    owned_key = proj_owned[:, query_cols : query_cols + key_columns]
    owned_value = proj_owned[:, query_cols + key_columns :]
    (
        summed_former,
        summed_query,
        summed_key,
        summed_value,
        summed_out,
        summed_latter,
        summed_inbound,
        summed_outbound,
    ) = (
        lax.psum(owned_former.astype(jnp.bfloat16), "rep").astype(jnp.float32),
        lax.psum(owned_query.astype(jnp.bfloat16), "rep").astype(jnp.float32),
        lax.psum(owned_key.astype(jnp.bfloat16), "rep").astype(jnp.float32),
        lax.psum(owned_value.astype(jnp.bfloat16), "rep").astype(jnp.float32),
        lax.psum(owned_out.astype(jnp.bfloat16), "rep").astype(jnp.float32),
        lax.psum(owned_latter.astype(jnp.bfloat16), "rep").astype(jnp.float32),
        lax.psum(inbound_grad.astype(jnp.bfloat16), "rep").astype(jnp.float32),
        lax.psum(outbound_grad.astype(jnp.bfloat16), "rep").astype(jnp.float32),
    )
    return (
        output,
        input_grad,
        summed_former,
        summed_query,
        summed_key,
        summed_value,
        summed_out,
        summed_latter,
        summed_inbound,
        summed_outbound,
    )


PAIR = [(0, 1), (1, 0)]


def swap(values, axis):
    return lax.ppermute(values, axis, PAIR)


def bf(values):
    return values.astype(jnp.bfloat16)


def f32(values):
    return values.astype(jnp.float32)


def dot(left, right):
    return jnp.dot(left, right, preferred_element_type=jnp.float32)


def dot_nt(left, right):
    return lax.dot_general(left, right, (((1,), (1,)), ((), ())), preferred_element_type=jnp.float32)


def dot_tn(left, right):
    return lax.dot_general(left, right, (((0,), (0,)), ((), ())), preferred_element_type=jnp.float32)


def ein(spec, left, right):
    return jnp.einsum(spec, left, right, preferred_element_type=jnp.float32)


def gather_group(rows):
    half = rows.shape[1] // 2
    first, second = rows[:, :half], rows[:, half:]
    first = jnp.stack([first, swap(first, "x")])
    second = jnp.stack([second, swap(second, "y")])
    first = jnp.stack([first, swap(first, "y")])
    second = jnp.stack([second, swap(second, "x")], axis=1)
    halves = []
    for part in (first, second):
        both = jnp.stack([part, swap(part, "core")])
        halves.append(both.reshape((8,) + rows.shape[:1] + (half,)))
    return halves


def scatter_group(parts):
    half = parts.shape[-1] // 2
    kept = bf(f32(parts[0]) + f32(swap(parts[1], "core")))
    first, second = kept[..., :half], kept[..., half:]
    first = bf(f32(first[:, 0]) + f32(swap(first[:, 1], "x")))
    second = bf(f32(second[0]) + f32(swap(second[1], "y")))
    first = f32(first[0]) + f32(swap(first[1], "y"))
    second = f32(second[0]) + f32(swap(second[1], "x"))
    return jnp.concatenate([first, second], axis=1)


def scatter_group_by_tokens(parts):
    half = parts.shape[-2] // 2
    first, second = parts[..., :half, :], parts[..., half:, :]
    first = bf(f32(first[0]) + f32(swap(first[1], "core")))
    second = bf(f32(second[0]) + f32(swap(second[1], "core")))
    first = bf(f32(first[:, 0]) + f32(swap(first[:, 1], "x")))
    second = bf(f32(second[0]) + f32(swap(second[1], "y")))
    first = f32(first[0]) + f32(swap(first[1], "y"))
    second = f32(second[0]) + f32(swap(second[1], "x"))
    return jnp.concatenate([first, second], axis=0)


def per_device_split(
    tokens,
    positions,
    routes,
    gates,
    cotangent,
    attn_gain,
    w_query,
    key_weight,
    value_weight,
    w_out,
    ffn_gain,
    w_gate_up,
    w_down,
):
    length, width = tokens.shape
    half_width = width // 2
    heads = KEY_VALUE_HEADS // 2
    grouped = QUERY_HEADS // KEY_VALUE_HEADS
    q_cols = heads * grouped * HEAD_DIM
    k_cols = heads * HEAD_DIM
    here = lax.axis_index("x")
    member = lax.axis_index("y") * 2 + lax.axis_index("core")
    expert = here * 4 + member

    def mine(values, axis):
        size = values.shape[axis] // 2
        return lax.dynamic_slice_in_dim(values, here * size, size, axis)

    def other(values, axis):
        size = values.shape[axis] // 2
        return lax.dynamic_slice_in_dim(values, (1 - here) * size, size, axis)

    def ordered(own, received, axis):
        return jnp.where(
            here == 0,
            jnp.concatenate([own, received], axis),
            jnp.concatenate([received, own], axis),
        )

    def turned(values):
        return jnp.concatenate([values[length:], values[:length]], axis=0)

    inputs = f32(tokens)
    inverse = lax.rsqrt(jnp.mean(inputs * inputs, axis=-1, keepdims=True) + RMS_EPS)
    own_cols = mine(tokens, 1)
    their_cols = swap(other(tokens, 1), "x")
    facts = jnp.concatenate(
        [
            gates.T,
            f32(routes).T,
            f32(positions)[None],
            inverse.T,
            f32(ffn_gain).reshape(-1, length),
        ],
        axis=0,
    )
    facts = jnp.pad(facts, ((0, -facts.shape[0] % 8), (0, 0)))
    their_facts = swap(facts, "x")
    facts_pair = jnp.stack([facts, their_facts])
    facts_quad = jnp.stack([facts_pair, swap(facts_pair, "y")])
    facts_all = jnp.stack([facts_quad, swap(facts_quad, "core")]).reshape((8,) + facts.shape)

    gain_one = f32(attn_gain)
    normed = jnp.concatenate(
        [
            bf(f32(own_cols) * inverse * gain_one),
            bf(f32(their_cols) * their_facts[5][:, None] * gain_one),
        ],
        axis=0,
    )
    partial = [dot(normed, w) for w in (w_query, key_weight, value_weight)]
    leaving = jnp.concatenate([bf(other(p, 1)) for p in partial], axis=1)
    arrived = turned(swap(leaving, "x"))
    kept = jnp.concatenate([mine(p, 1) for p in partial], axis=1) + f32(arrived)
    place = jnp.stack([facts[4], their_facts[4]])
    half_dim = HEAD_DIM // 2
    frequency = ROPE_BASE ** (-(2.0 * jnp.arange(half_dim, dtype=jnp.float32)) / HEAD_DIM)
    angles = place[:, :, None] * frequency
    cosine, sinusoid = jnp.cos(angles)[:, :, None, :], jnp.sin(angles)[:, :, None, :]
    q = bf(apply_rotary(kept[:, :q_cols].reshape(2, length, -1, HEAD_DIM), cosine, sinusoid))
    k = bf(
        apply_rotary(
            kept[:, q_cols : q_cols + k_cols].reshape(2, length, -1, HEAD_DIM), cosine, sinusoid
        )
    )
    v = bf(kept[:, q_cols + k_cols :]).reshape(2, length, heads, HEAD_DIM)
    q = q.reshape(2, length, heads, grouped, HEAD_DIM)
    causal = jnp.arange(length)[:, None] >= jnp.arange(length)[None, :]
    scores = jnp.where(causal, ATT_MULT * ein("sqhgd,skhd->shgqk", q, k), -1e30)
    probs = jax.nn.softmax(scores, axis=-1)
    probs_low = bf(probs)
    attended = bf(ein("shgqk,skhd->sqhgd", probs_low, v)).reshape(2 * length, q_cols)
    branch = dot(attended, w_out)
    hidden = inputs + RES_MULT * (branch[:length] + f32(swap(bf(branch[length:]), "x")))
    gain_rows = half_width // length
    gain_two = ordered(
        facts[6 : 6 + gain_rows].reshape(-1), their_facts[6 : 6 + gain_rows].reshape(-1), 0
    )
    inverse_two = lax.rsqrt(jnp.mean(hidden * hidden, axis=-1, keepdims=True) + RMS_EPS)
    second = bf(hidden * inverse_two * gain_two)

    match = f32(facts_all[:, 2:4] == f32(expert))
    taken = jnp.sum(match, axis=1)
    gate = jnp.sum(facts_all[:, 0:2] * match, axis=1)
    rank = dot(bf(taken), bf(jnp.arange(length)[:, None] < jnp.arange(length)[None, :]))
    slots = jnp.arange(CAP, dtype=jnp.float32)
    pick = bf((rank[:, None, :] == slots[None, :, None]) & (taken[:, None, :] > 0))
    w_in = lax.dynamic_index_in_dim(w_gate_up, member, 0, keepdims=False)
    w_back = lax.dynamic_index_in_dim(w_down, member, 0, keepdims=False)

    def dispatch(values):
        return bf(ein("sct,std->scd", pick, values)).reshape(8 * CAP, -1)

    def undispatch(values):
        return ein("sct,scd->std", pick, values.reshape(8, CAP, -1))

    upstream = f32(cotangent)
    out_grad = jnp.concatenate(
        [dispatch(bf(gate[:, :, None] * (RES_MULT * f32(part)))) for part in gather_group(cotangent)],
        axis=1,
    )
    act_grad = dot_nt(out_grad, w_back)
    rows = jnp.concatenate([dispatch(part) for part in gather_group(second)], axis=1)
    gate_up = dot(rows, w_in)
    front, back = gate_up[:, :F], gate_up[:, F:]
    sigmoid = jax.nn.sigmoid(front)
    silu = front * sigmoid
    activated = bf(silu * back)
    inner = jnp.concatenate(
        [
            bf(act_grad * back * (sigmoid * (1.0 + front * (1.0 - sigmoid)))),
            bf(act_grad * silu),
        ],
        axis=1,
    )
    rows_grad = bf(dot_nt(inner, w_in))
    shape = (2, 2, 2, length, width)
    second_grad = scatter_group(bf(undispatch(rows_grad)).reshape(shape))
    grad_down = bf(dot_tn(activated, out_grad))
    grad_gate_up = bf(dot_tn(rows, inner))
    expert_out = bf(dot(activated, w_back))
    combined = scatter_group_by_tokens(bf(gate[:, :, None] * undispatch(expert_out)).reshape(shape))

    cotan = second_grad * gain_two
    hidden_grad = (
        upstream
        + inverse_two * cotan
        - hidden * inverse_two**3 * jnp.mean(cotan * hidden, axis=-1, keepdims=True)
    )
    gain_grad = jnp.sum(second_grad * hidden * inverse_two, axis=0, keepdims=True)
    branch_grad = bf(RES_MULT * hidden_grad)
    both = jnp.concatenate([branch_grad, bf(jnp.pad(gain_grad, ((0, 15), (0, 0))))], axis=0)
    theirs = swap(both, "x")
    held, _ = lax.optimization_barrier((hidden, theirs))
    output = bf(held + RES_MULT * combined)
    grad_ffn = mine(gain_grad + f32(theirs[length : length + 1]), 1)
    branch_pair = jnp.concatenate([branch_grad, theirs[:length]], axis=0)
    att_grad = bf(dot_nt(branch_pair, w_out)).reshape(2, length, heads, grouped, HEAD_DIM)
    grad_out = bf(dot_tn(attended, branch_pair))
    probs_grad = ein("sqhgd,skhd->shgqk", att_grad, v)
    inner_sum = jnp.sum(probs * probs_grad, axis=-1, keepdims=True)
    score_grad = bf(probs * (probs_grad - inner_sum))
    v_grad = bf(ein("shgqk,sqhgd->skhd", probs_low, att_grad)).reshape(2 * length, -1)
    q_grad = ATT_MULT * ein("shgqk,skhd->sqhgd", score_grad, k)
    k_grad = ATT_MULT * ein("shgqk,sqhgd->skhd", score_grad, q)
    q_grad = bf(apply_rotary(q_grad.reshape(2, length, -1, HEAD_DIM), cosine, -sinusoid))
    k_grad = bf(apply_rotary(k_grad, cosine, -sinusoid))
    turned_grad = jnp.concatenate(
        [q_grad.reshape(2 * length, -1), k_grad.reshape(2 * length, -1), v_grad], axis=1
    )
    their_grad = turned(swap(turned_grad, "x"))
    pieces = []
    for lo, hi in ((0, q_cols), (q_cols, q_cols + k_cols), (q_cols + k_cols, q_cols + 2 * k_cols)):
        pieces.append(ordered(turned_grad[:, lo:hi], their_grad[:, lo:hi], 1))
    normed_grad = (
        dot_nt(pieces[0], w_query)
        + dot_nt(pieces[1], key_weight)
        + dot_nt(pieces[2], value_weight)
    )
    weighted = normed_grad * gain_one
    full = ordered(weighted[:length], f32(swap(bf(weighted[length:]), "x")), 1)
    input_grad = bf(
        hidden_grad
        + inverse * full
        - inputs * inverse**3 * jnp.mean(full * inputs, axis=-1, keepdims=True)
    )
    scaled = jnp.concatenate(
        [f32(own_cols) * inverse, f32(their_cols) * their_facts[5][:, None]], axis=0
    )
    grad_attn = jnp.sum(normed_grad * scaled, axis=0, keepdims=True)
    grads = [bf(dot_tn(normed, piece)) for piece in pieces]
    return (output, input_grad, grad_attn, grad_ffn, grads, grad_out, grad_gate_up, grad_down)


def apart(values, step, before):
    return lax.optimization_barrier((values, before[step]))[0] if step in before else values


def over_z(part, before):
    chips = lax.axis_size("z")
    if chips != 4:
        return lax.psum(part, "z")
    inner = (lax.axis_index("z") + 1) // 2 == 1
    came = apart(lax.ppermute(part, "z", [(0, 1), (3, 2)]), 1, before)
    held = bf(f32(part) + f32(came))
    came = apart(lax.ppermute(held, "z", [(1, 2), (2, 1)]), 2, before)
    total = bf(f32(held) + f32(came))
    came = apart(lax.ppermute(total, "z", [(1, 0), (2, 3)]), 3, before)
    final = jnp.where(inner, total, came)
    before.update({1: held, 2: total, 3: final})
    return final


def copies(part):
    across = swap(part, "y")
    return [part, swap(part, "core"), across, swap(across, "core")]


def quarter(values):
    for axis in ("core", "y"):
        rows = values.shape[0] // 2
        at = lax.axis_index(axis)
        own = lax.dynamic_slice_in_dim(values, at * rows, rows, 0)
        out = lax.dynamic_slice_in_dim(values, (1 - at) * rows, rows, 0)
        values = bf(f32(own) + f32(swap(out, axis)))
    return values


PIECE = 256


def put_piece(places, parts, whole, rows, block):
    size, width = parts[0].shape
    step = size // 4

    def kernel(places_ref, *refs):
        for flip in range(4):
            refs[-1][places_ref[flip]] = refs[flip][...].astype(jnp.float32)

    part_spec = pl.BlockSpec((step, width), lambda at, places: (at, 0))
    more = [] if whole is None else [whole]
    return pl.pallas_call(
        kernel,
        out_shape=jax.ShapeDtypeStruct((4, rows, width), jnp.float32),
        grid_spec=pltpu.PrefetchScalarGridSpec(
            num_scalar_prefetch=1,
            grid=(4,),
            in_specs=[part_spec] * 4 + [pl.BlockSpec(memory_space=pl.ANY)] * len(more),
            out_specs=pl.BlockSpec(
                (4, step, width), lambda at, places: (0, block * 4 + at, 0)
            ),
        ),
        input_output_aliases={5: 0} if more else {},
    )(places, *parts, *more)


def put_rows(places, parts, widths):
    size, width = parts[0].shape
    step = size // 4

    def kernel(places_ref, *refs):
        for flip in range(4):
            at = 0
            for out, cut in zip(refs[4:], widths):
                out[places_ref[flip]] = refs[flip][:, at : at + cut].astype(jnp.float32)
                at += cut

    outs = pl.pallas_call(
        kernel,
        out_shape=[jax.ShapeDtypeStruct((4, size, cut), jnp.float32) for cut in widths],
        grid_spec=pltpu.PrefetchScalarGridSpec(
            num_scalar_prefetch=1,
            grid=(4,),
            in_specs=[pl.BlockSpec((step, width), lambda at, places: (at, 0))] * 4,
            out_specs=[
                pl.BlockSpec((4, step, cut), lambda at, places: (0, at, 0)) for cut in widths
            ],
        ),
    )(places, *parts)
    return [out.reshape(4 * size, cut) for out, cut in zip(outs, widths)]


def reduced_step(*arrays):
    output, input_grad, grad_attn, grad_ffn, grads, grad_out, grad_gate_up, grad_down = (
        per_device_split(*arrays)
    )
    core, row = lax.axis_index("core"), lax.axis_index("y")
    flips = jnp.arange(4, dtype=jnp.int32)
    experts = (row * 2 + core) ^ flips
    quarters = (core ^ (flips & 1)) * 2 + (row ^ (flips >> 1))
    sums, before = [], {}
    for values in (grad_down, grad_gate_up):
        whole = None
        for at in range(0, values.shape[0], PIECE):
            total = over_z(values[at : at + PIECE], before)
            parts = copies(total)
            rows, block = values.shape[0], at // PIECE
            whole = put_piece(experts, parts, whole, rows, block)
        sums.append(whole)
    sum_down, sum_gate_up = sums

    def over_all(pieces):
        wide = jnp.concatenate(pieces, axis=1)
        parts = copies(over_z(quarter(wide), {}))
        return put_rows(quarters, parts, [p.shape[1] for p in pieces])

    gains = bf(jnp.concatenate([grad_attn, grad_ffn], axis=0)).T
    (sum_out,) = over_all([grad_out])
    *sum_proj, sum_gains = over_all(grads + [jnp.pad(gains, ((0, 0), (0, 126)))])
    return (
        output,
        input_grad,
        sum_gains[:, 0],
        *sum_proj,
        sum_out,
        sum_gains[:, 1],
        sum_gate_up,
        sum_down,
    )


def solution(mesh):
    replicas, shards = mesh.devices.shape
    if shards == 2 and EXPERTS == 8 and replicas % 4 == 0:
        split = jax.sharding.Mesh(
            mesh.devices.reshape(replicas // 4, 2, 2, 2), ("z", "y", "core", "x")
        )
        step = mapped(reduced_step, split, ("z", "y", "core", "x"), "x")
        return step
    return mapped(per_device, mesh, ("rep", "shard"), "shard")


def mapped(step, mesh, every, shard):
    in_specs = (
        P(every, None),
        P(every),
        P(every, None),
        P(every, None),
        P(every, None),
        P(shard),
        P(shard, None),
        P(shard, None),
        P(shard, None),
        P(shard, None),
        P(shard),
        P(shard, None, None),
        P(shard, None, None),
    )
    out_specs = (
        P(every, None),
        P(every, None),
        P(shard),
        P(shard, None),
        P(shard, None),
        P(shard, None),
        P(shard, None),
        P(shard),
        P(shard, None, None),
        P(shard, None, None),
    )
    return jax.shard_map(step, mesh=mesh, in_specs=in_specs, out_specs=out_specs, check_vma=False)
```

```python
import jax
import jax.numpy as jnp
from jax import lax
from jax.experimental import pallas as pl
from jax.experimental.pallas import tpu as pltpu
from jax.sharding import PartitionSpec as P

QUERY_HEADS = 16
KEY_VALUE_HEADS = 8
HEAD_DIM = 64
F = 512
EXPERTS = 8
TOP = 2
CAP = 48


RMS_EPS = 1e-06
RES_MULT = 0.22
ATT_MULT = 0.015625
ROPE_BASE = 10000.0


def rms_norm(values, norm_gain):
    inverse = lax.rsqrt(jnp.mean(values * values, axis=-1, keepdims=True) + RMS_EPS)
    return values * inverse * norm_gain


def rope_tables(positions):
    half_dim = HEAD_DIM // 2
    frequency = ROPE_BASE ** (-(2.0 * jnp.arange(half_dim, dtype=jnp.float32)) / HEAD_DIM)
    angles = positions.astype(jnp.float32)[:, None] * frequency[None, :]
    return (jnp.cos(angles)[:, None, :], jnp.sin(angles)[:, None, :])


def apply_rotary(values, cosine_table, sinusoid_table):
    half_dim = values.shape[-1] // 2
    front_half = values[..., :half_dim]
    back_half = values[..., half_dim:]
    return jnp.concatenate(
        [
            front_half * cosine_table - back_half * sinusoid_table,
            back_half * cosine_table + front_half * sinusoid_table,
        ],
        axis=-1,
    )


def swiglu(gate_up):
    return jax.nn.silu(gate_up[..., :F]) * gate_up[..., F:]


def slot_table(routes):
    flat_routes = routes.reshape(-1)
    onehot = (flat_routes[:, None] == jnp.arange(EXPERTS, dtype=jnp.int32)[None, :]).astype(
        jnp.int32
    )
    before = jnp.cumsum(onehot, axis=0) - onehot
    ranked = jnp.sum(before * onehot, axis=1)
    slot_index = flat_routes * CAP + ranked
    owners = jnp.arange(flat_routes.shape[0], dtype=jnp.int32) // TOP
    sources = jnp.zeros((EXPERTS * CAP,), jnp.int32).at[slot_index].set(owners)
    filled = jnp.zeros((EXPERTS * CAP,), jnp.float32).at[slot_index].set(1.0)
    return (slot_index, sources, filled)


def masked_scores(query_head_rows, key_head_rows, causal):
    scores = ATT_MULT * jnp.einsum(
        "qhgd,khd->hgqk", query_head_rows, key_head_rows, preferred_element_type=jnp.float32
    )
    return jnp.where(causal, scores, -1e30)


def per_device(
    tokens,
    positions,
    routes,
    gates,
    cotangent,
    attn_gain,
    w_query,
    key_weight,
    value_weight,
    w_out,
    ffn_gain,
    w_gate_up,
    w_down,
):
    sequence_length = tokens.shape[0]
    model_width = tokens.shape[1]
    heads_per_group = QUERY_HEADS // KEY_VALUE_HEADS
    cosine_table, sinusoid_table = rope_tables(positions)
    causal = jnp.arange(sequence_length)[:, None] >= jnp.arange(sequence_length)[None, :]
    gain_one, full_query, full_key, full_value, full_out, gain_two = (
        lax.all_gather(attn_gain, "shard", axis=0, tiled=True),
        lax.all_gather(w_query, "shard", axis=0, tiled=True),
        lax.all_gather(key_weight, "shard", axis=0, tiled=True),
        lax.all_gather(value_weight, "shard", axis=0, tiled=True),
        lax.all_gather(w_out, "shard", axis=0, tiled=True),
        lax.all_gather(ffn_gain, "shard", axis=0, tiled=True),
    )
    inputs = tokens.astype(jnp.float32)
    normalized_input, norm_pull = jax.vjp(rms_norm, inputs, gain_one.astype(jnp.float32))
    normed_low = normalized_input.astype(jnp.bfloat16)
    query_proj = jnp.dot(normed_low, full_query, preferred_element_type=jnp.float32).reshape(
        sequence_length, QUERY_HEADS, HEAD_DIM
    )
    key_proj = jnp.dot(normed_low, full_key, preferred_element_type=jnp.float32).reshape(
        sequence_length, KEY_VALUE_HEADS, HEAD_DIM
    )
    value_head_rows = (
        jnp.dot(normed_low, full_value, preferred_element_type=jnp.float32)
        .astype(jnp.bfloat16)
        .reshape(sequence_length, KEY_VALUE_HEADS, HEAD_DIM)
    )
    query_head_rows = (
        apply_rotary(query_proj, cosine_table, sinusoid_table)
        .astype(jnp.bfloat16)
        .reshape(sequence_length, KEY_VALUE_HEADS, heads_per_group, HEAD_DIM)
    )
    key_head_rows = apply_rotary(key_proj, cosine_table, sinusoid_table).astype(jnp.bfloat16)
    scores = masked_scores(query_head_rows, key_head_rows, causal)
    top_score = jnp.max(scores, axis=-1, keepdims=True)
    log_total = top_score + jnp.log(jnp.sum(jnp.exp(scores - top_score), axis=-1, keepdims=True))
    probs_low = jnp.exp(scores - log_total).astype(jnp.bfloat16)
    attended = jnp.einsum(
        "hgqk,khd->qhgd", probs_low, value_head_rows, preferred_element_type=jnp.float32
    )
    attended = attended.reshape(sequence_length, QUERY_HEADS * HEAD_DIM).astype(jnp.bfloat16)
    branch = jnp.dot(attended, full_out, preferred_element_type=jnp.float32)
    hidden = inputs + RES_MULT * branch
    second, second_pull = jax.vjp(rms_norm, hidden, gain_two.astype(jnp.float32))
    second_low = second.astype(jnp.bfloat16)
    slot_index, sources, filled = slot_table(routes)
    dispatched = (second_low[sources] * filled[:, None].astype(jnp.bfloat16)).reshape(
        EXPERTS, CAP, model_width
    )
    received = lax.all_to_all(dispatched, "shard", split_axis=0, concat_axis=1, tiled=True)
    gate_up = jnp.einsum("ecd,edf->ecf", received, w_gate_up, preferred_element_type=jnp.float32)
    activated, act_pull = jax.vjp(swiglu, gate_up)
    act_low = activated.astype(jnp.bfloat16)
    expert_out = jnp.einsum(
        "ecf,efd->ecd", act_low, w_down, preferred_element_type=jnp.float32
    ).astype(jnp.bfloat16)
    returned = lax.all_to_all(expert_out, "shard", split_axis=1, concat_axis=0, tiled=True).reshape(
        EXPERTS * CAP, model_width
    )
    picked = returned[slot_index].reshape(sequence_length, TOP, model_width).astype(jnp.float32)
    combined = jnp.sum(gates[:, :, None] * picked, axis=1)
    output = (hidden + RES_MULT * combined).astype(jnp.bfloat16)
    upstream = cotangent.astype(jnp.float32)
    route_grad = (gates[:, :, None] * (RES_MULT * upstream)[:, None, :]).astype(jnp.bfloat16)
    route_grad = route_grad.reshape(sequence_length * TOP, model_width)
    out_grad = jnp.zeros((EXPERTS * CAP, model_width), jnp.bfloat16).at[slot_index].set(route_grad)
    out_grad = out_grad.reshape(EXPERTS, CAP, model_width)
    grad_arrived = lax.all_to_all(out_grad, "shard", split_axis=0, concat_axis=1, tiled=True)
    outbound_grad = jnp.einsum(
        "ecf,ecd->efd", act_low, grad_arrived, preferred_element_type=jnp.float32
    )
    act_grad = jnp.einsum("ecd,efd->ecf", grad_arrived, w_down, preferred_element_type=jnp.float32)
    inner_grad = act_pull(act_grad)[0].astype(jnp.bfloat16)
    inbound_grad = jnp.einsum(
        "ecd,ecf->edf", received, inner_grad, preferred_element_type=jnp.float32
    )
    rows_grad = jnp.einsum(
        "ecf,edf->ecd", inner_grad, w_gate_up, preferred_element_type=jnp.float32
    ).astype(jnp.bfloat16)
    rows_back = lax.all_to_all(rows_grad, "shard", split_axis=1, concat_axis=0, tiled=True).reshape(
        EXPERTS * CAP, model_width
    )
    second_grad = jnp.sum(
        rows_back[slot_index].reshape(sequence_length, TOP, model_width).astype(jnp.float32), axis=1
    )
    hidden_part, grad_latter = second_pull(second_grad)
    hidden_grad = upstream + hidden_part
    full_query, full_key, full_value, full_out = (
        lax.all_gather(w_query, "shard", axis=0, tiled=True),
        lax.all_gather(key_weight, "shard", axis=0, tiled=True),
        lax.all_gather(value_weight, "shard", axis=0, tiled=True),
        lax.all_gather(w_out, "shard", axis=0, tiled=True),
    )
    branch_grad = (RES_MULT * hidden_grad).astype(jnp.bfloat16)
    attended_gradient = jnp.dot(branch_grad, full_out.T, preferred_element_type=jnp.float32).astype(
        jnp.bfloat16
    )
    attended_gradient = attended_gradient.reshape(
        sequence_length, KEY_VALUE_HEADS, heads_per_group, HEAD_DIM
    )
    rescored = masked_scores(query_head_rows, key_head_rows, causal)
    probs = jnp.exp(rescored - log_total)
    probs_again = probs.astype(jnp.bfloat16)
    probs_grad = jnp.einsum(
        "qhgd,khd->hgqk", attended_gradient, value_head_rows, preferred_element_type=jnp.float32
    )
    row_inner = jnp.sum(probs * probs_grad, axis=-1, keepdims=True)
    score_grad = (probs * (probs_grad - row_inner)).astype(jnp.bfloat16)
    value_gradient = jnp.einsum(
        "hgqk,qhgd->khd", probs_again, attended_gradient, preferred_element_type=jnp.float32
    )
    value_gradient = value_gradient.astype(jnp.bfloat16).reshape(
        sequence_length, KEY_VALUE_HEADS * HEAD_DIM
    )
    query_turned = ATT_MULT * jnp.einsum(
        "hgqk,khd->qhgd", score_grad, key_head_rows, preferred_element_type=jnp.float32
    )
    rotated_keys = ATT_MULT * jnp.einsum(
        "hgqk,qhgd->khd", score_grad, query_head_rows, preferred_element_type=jnp.float32
    )
    query_grad = (
        apply_rotary(
            query_turned.reshape(sequence_length, QUERY_HEADS, HEAD_DIM),
            cosine_table,
            -sinusoid_table,
        )
        .astype(jnp.bfloat16)
        .reshape(sequence_length, QUERY_HEADS * HEAD_DIM)
    )
    key_grad = (
        apply_rotary(rotated_keys, cosine_table, -sinusoid_table)
        .astype(jnp.bfloat16)
        .reshape(sequence_length, KEY_VALUE_HEADS * HEAD_DIM)
    )
    normed_grad = jnp.dot(query_grad, full_query.T, preferred_element_type=jnp.float32)
    normed_grad = normed_grad + jnp.dot(key_grad, full_key.T, preferred_element_type=jnp.float32)
    normed_grad = normed_grad + jnp.dot(
        value_gradient, full_value.T, preferred_element_type=jnp.float32
    )
    input_part, grad_former = norm_pull(normed_grad)
    input_grad = (hidden_grad + input_part).astype(jnp.bfloat16)
    projected = jnp.concatenate([query_grad, key_grad, value_gradient], axis=1)
    proj_grad = jnp.dot(attended.T, branch_grad, preferred_element_type=jnp.float32)
    proj_owned = lax.psum_scatter(
        jnp.dot(normed_low.T, projected, preferred_element_type=jnp.float32).astype(jnp.bfloat16),
        "shard",
        scatter_dimension=0,
        tiled=True,
    ).astype(jnp.float32)
    owned_out, owned_former, owned_latter = (
        lax.psum_scatter(
            proj_grad.astype(jnp.bfloat16), "shard", scatter_dimension=0, tiled=True
        ).astype(jnp.float32),
        lax.psum_scatter(
            grad_former.astype(jnp.bfloat16), "shard", scatter_dimension=0, tiled=True
        ).astype(jnp.float32),
        lax.psum_scatter(
            grad_latter.astype(jnp.bfloat16), "shard", scatter_dimension=0, tiled=True
        ).astype(jnp.float32),
    )
    query_cols = QUERY_HEADS * HEAD_DIM
    key_columns = KEY_VALUE_HEADS * HEAD_DIM
    owned_query = proj_owned[:, :query_cols]
    owned_key = proj_owned[:, query_cols : query_cols + key_columns]
    owned_value = proj_owned[:, query_cols + key_columns :]
    (
        summed_former,
        summed_query,
        summed_key,
        summed_value,
        summed_out,
        summed_latter,
        summed_inbound,
        summed_outbound,
    ) = (
        lax.psum(owned_former.astype(jnp.bfloat16), "rep").astype(jnp.float32),
        lax.psum(owned_query.astype(jnp.bfloat16), "rep").astype(jnp.float32),
        lax.psum(owned_key.astype(jnp.bfloat16), "rep").astype(jnp.float32),
        lax.psum(owned_value.astype(jnp.bfloat16), "rep").astype(jnp.float32),
        lax.psum(owned_out.astype(jnp.bfloat16), "rep").astype(jnp.float32),
        lax.psum(owned_latter.astype(jnp.bfloat16), "rep").astype(jnp.float32),
        lax.psum(inbound_grad.astype(jnp.bfloat16), "rep").astype(jnp.float32),
        lax.psum(outbound_grad.astype(jnp.bfloat16), "rep").astype(jnp.float32),
    )
    return (
        output,
        input_grad,
        summed_former,
        summed_query,
        summed_key,
        summed_value,
        summed_out,
        summed_latter,
        summed_inbound,
        summed_outbound,
    )


PAIR = [(0, 1), (1, 0)]


def swap(values, axis):
    return lax.ppermute(values, axis, PAIR)


def bf(values):
    return values.astype(jnp.bfloat16)


def f32(values):
    return values.astype(jnp.float32)


def dot(left, right):
    return jnp.dot(left, right, preferred_element_type=jnp.float32)


def dot_nt(left, right):
    return lax.dot_general(left, right, (((1,), (1,)), ((), ())), preferred_element_type=jnp.float32)


def dot_tn(left, right):
    return lax.dot_general(left, right, (((0,), (0,)), ((), ())), preferred_element_type=jnp.float32)


def ein(spec, left, right):
    return jnp.einsum(spec, left, right, preferred_element_type=jnp.float32)


def gather_group(rows):
    half = rows.shape[1] // 2
    first, second = rows[:, :half], rows[:, half:]
    first = jnp.stack([first, swap(first, "x")])
    second = jnp.stack([second, swap(second, "y")])
    first = jnp.stack([first, swap(first, "y")])
    second = jnp.stack([second, swap(second, "x")], axis=1)
    halves = []
    for part in (first, second):
        both = jnp.stack([part, swap(part, "c")])
        halves.append(both.reshape((8,) + rows.shape[:1] + (half,)))
    return halves


def scatter_group(parts):
    half = parts.shape[-1] // 2
    kept = bf(f32(parts[0]) + f32(swap(parts[1], "c")))
    first, second = kept[..., :half], kept[..., half:]
    first = bf(f32(first[:, 0]) + f32(swap(first[:, 1], "x")))
    second = bf(f32(second[0]) + f32(swap(second[1], "y")))
    first = f32(first[0]) + f32(swap(first[1], "y"))
    second = f32(second[0]) + f32(swap(second[1], "x"))
    return jnp.concatenate([first, second], axis=1)


def scatter_group_by_tokens(parts):
    half = parts.shape[-2] // 2
    first, second = parts[..., :half, :], parts[..., half:, :]
    first = bf(f32(first[0]) + f32(swap(first[1], "c")))
    second = bf(f32(second[0]) + f32(swap(second[1], "c")))
    first = bf(f32(first[:, 0]) + f32(swap(first[:, 1], "x")))
    second = bf(f32(second[0]) + f32(swap(second[1], "y")))
    first = f32(first[0]) + f32(swap(first[1], "y"))
    second = f32(second[0]) + f32(swap(second[1], "x"))
    return jnp.concatenate([first, second], axis=0)


def per_device_split(
    tokens,
    positions,
    routes,
    gates,
    cotangent,
    attn_gain,
    w_query,
    key_weight,
    value_weight,
    w_out,
    ffn_gain,
    w_gate_up,
    w_down,
):
    length, width = tokens.shape
    half_width = width // 2
    heads = KEY_VALUE_HEADS // 2
    grouped = QUERY_HEADS // KEY_VALUE_HEADS
    q_cols = heads * grouped * HEAD_DIM
    k_cols = heads * HEAD_DIM
    here = lax.axis_index("x")
    member = lax.axis_index("y") * 2 + lax.axis_index("c")
    expert = here * 4 + member

    def mine(values, axis):
        size = values.shape[axis] // 2
        return lax.dynamic_slice_in_dim(values, here * size, size, axis)

    def other(values, axis):
        size = values.shape[axis] // 2
        return lax.dynamic_slice_in_dim(values, (1 - here) * size, size, axis)

    def ordered(own, received, axis):
        return jnp.where(
            here == 0,
            jnp.concatenate([own, received], axis),
            jnp.concatenate([received, own], axis),
        )

    def turned(values):
        return jnp.concatenate([values[length:], values[:length]], axis=0)

    inputs = f32(tokens)
    inverse = lax.rsqrt(jnp.mean(inputs * inputs, axis=-1, keepdims=True) + RMS_EPS)
    own_cols = mine(tokens, 1)
    their_cols = swap(other(tokens, 1), "x")
    facts = jnp.concatenate(
        [
            gates.T,
            f32(routes).T,
            f32(positions)[None],
            inverse.T,
            f32(ffn_gain).reshape(-1, length),
        ],
        axis=0,
    )
    facts = jnp.pad(facts, ((0, -facts.shape[0] % 8), (0, 0)))
    their_facts = swap(facts, "x")
    facts_pair = jnp.stack([facts, their_facts])
    facts_quad = jnp.stack([facts_pair, swap(facts_pair, "y")])
    facts_all = jnp.stack([facts_quad, swap(facts_quad, "c")]).reshape((8,) + facts.shape)

    gain_one = f32(attn_gain)
    normed = jnp.concatenate(
        [
            bf(f32(own_cols) * inverse * gain_one),
            bf(f32(their_cols) * their_facts[5][:, None] * gain_one),
        ],
        axis=0,
    )
    partial = [dot(normed, w) for w in (w_query, key_weight, value_weight)]
    leaving = jnp.concatenate([bf(other(p, 1)) for p in partial], axis=1)
    arrived = turned(swap(leaving, "x"))
    kept = jnp.concatenate([mine(p, 1) for p in partial], axis=1) + f32(arrived)
    place = jnp.stack([facts[4], their_facts[4]])
    half_dim = HEAD_DIM // 2
    frequency = ROPE_BASE ** (-(2.0 * jnp.arange(half_dim, dtype=jnp.float32)) / HEAD_DIM)
    angles = place[:, :, None] * frequency
    cosine, sinusoid = jnp.cos(angles)[:, :, None, :], jnp.sin(angles)[:, :, None, :]
    q = bf(apply_rotary(kept[:, :q_cols].reshape(2, length, -1, HEAD_DIM), cosine, sinusoid))
    k = bf(
        apply_rotary(
            kept[:, q_cols : q_cols + k_cols].reshape(2, length, -1, HEAD_DIM), cosine, sinusoid
        )
    )
    v = bf(kept[:, q_cols + k_cols :]).reshape(2, length, heads, HEAD_DIM)
    q = q.reshape(2, length, heads, grouped, HEAD_DIM)
    causal = jnp.arange(length)[:, None] >= jnp.arange(length)[None, :]
    scores = jnp.where(causal, ATT_MULT * ein("sqhgd,skhd->shgqk", q, k), -1e30)
    probs = jax.nn.softmax(scores, axis=-1)
    probs_low = bf(probs)
    attended = bf(ein("shgqk,skhd->sqhgd", probs_low, v)).reshape(2 * length, q_cols)
    branch = dot(attended, w_out)
    hidden = inputs + RES_MULT * (branch[:length] + f32(swap(bf(branch[length:]), "x")))
    gain_rows = half_width // length
    gain_two = ordered(
        facts[6 : 6 + gain_rows].reshape(-1), their_facts[6 : 6 + gain_rows].reshape(-1), 0
    )
    inverse_two = lax.rsqrt(jnp.mean(hidden * hidden, axis=-1, keepdims=True) + RMS_EPS)
    second = bf(hidden * inverse_two * gain_two)

    match = f32(facts_all[:, 2:4] == f32(expert))
    taken = jnp.sum(match, axis=1)
    gate = jnp.sum(facts_all[:, 0:2] * match, axis=1)
    rank = dot(bf(taken), bf(jnp.arange(length)[:, None] < jnp.arange(length)[None, :]))
    slots = jnp.arange(CAP, dtype=jnp.float32)
    pick = bf((rank[:, None, :] == slots[None, :, None]) & (taken[:, None, :] > 0))
    w_in = lax.dynamic_index_in_dim(w_gate_up, member, 0, keepdims=False)
    w_back = lax.dynamic_index_in_dim(w_down, member, 0, keepdims=False)

    def dispatch(values):
        return bf(ein("sct,std->scd", pick, values)).reshape(8 * CAP, -1)

    def undispatch(values):
        return ein("sct,scd->std", pick, values.reshape(8, CAP, -1))

    upstream = f32(cotangent)
    out_grad = jnp.concatenate(
        [dispatch(bf(gate[:, :, None] * (RES_MULT * f32(part)))) for part in gather_group(cotangent)],
        axis=1,
    )
    act_grad = dot_nt(out_grad, w_back)
    rows = jnp.concatenate([dispatch(part) for part in gather_group(second)], axis=1)
    gate_up = dot(rows, w_in)
    front, back = gate_up[:, :F], gate_up[:, F:]
    sigmoid = jax.nn.sigmoid(front)
    silu = front * sigmoid
    activated = bf(silu * back)
    inner = jnp.concatenate(
        [
            bf(act_grad * back * (sigmoid * (1.0 + front * (1.0 - sigmoid)))),
            bf(act_grad * silu),
        ],
        axis=1,
    )
    rows_grad = bf(dot_nt(inner, w_in))
    shape = (2, 2, 2, length, width)
    second_grad = scatter_group(bf(undispatch(rows_grad)).reshape(shape))
    grad_down = bf(dot_tn(activated, out_grad))
    grad_gate_up = bf(dot_tn(rows, inner))
    expert_out = bf(dot(activated, w_back))
    combined = scatter_group_by_tokens(bf(gate[:, :, None] * undispatch(expert_out)).reshape(shape))

    cotan = second_grad * gain_two
    hidden_grad = (
        upstream
        + inverse_two * cotan
        - hidden * inverse_two**3 * jnp.mean(cotan * hidden, axis=-1, keepdims=True)
    )
    gain_grad = jnp.sum(second_grad * hidden * inverse_two, axis=0, keepdims=True)
    branch_grad = bf(RES_MULT * hidden_grad)
    both = jnp.concatenate([branch_grad, bf(jnp.pad(gain_grad, ((0, 15), (0, 0))))], axis=0)
    theirs = swap(both, "x")
    held, _ = lax.optimization_barrier((hidden, theirs))
    output = bf(held + RES_MULT * combined)
    grad_ffn = mine(gain_grad + f32(theirs[length : length + 1]), 1)
    branch_pair = jnp.concatenate([branch_grad, theirs[:length]], axis=0)
    att_grad = bf(dot_nt(branch_pair, w_out)).reshape(2, length, heads, grouped, HEAD_DIM)
    grad_out = bf(dot_tn(attended, branch_pair))
    probs_grad = ein("sqhgd,skhd->shgqk", att_grad, v)
    inner_sum = jnp.sum(probs * probs_grad, axis=-1, keepdims=True)
    score_grad = bf(probs * (probs_grad - inner_sum))
    v_grad = bf(ein("shgqk,sqhgd->skhd", probs_low, att_grad)).reshape(2 * length, -1)
    q_grad = ATT_MULT * ein("shgqk,skhd->sqhgd", score_grad, k)
    k_grad = ATT_MULT * ein("shgqk,sqhgd->skhd", score_grad, q)
    q_grad = bf(apply_rotary(q_grad.reshape(2, length, -1, HEAD_DIM), cosine, -sinusoid))
    k_grad = bf(apply_rotary(k_grad, cosine, -sinusoid))
    turned_grad = jnp.concatenate(
        [q_grad.reshape(2 * length, -1), k_grad.reshape(2 * length, -1), v_grad], axis=1
    )
    their_grad = turned(swap(turned_grad, "x"))
    pieces = []
    for lo, hi in ((0, q_cols), (q_cols, q_cols + k_cols), (q_cols + k_cols, q_cols + 2 * k_cols)):
        pieces.append(ordered(turned_grad[:, lo:hi], their_grad[:, lo:hi], 1))
    normed_grad = (
        dot_nt(pieces[0], w_query)
        + dot_nt(pieces[1], key_weight)
        + dot_nt(pieces[2], value_weight)
    )
    weighted = normed_grad * gain_one
    full = ordered(weighted[:length], f32(swap(bf(weighted[length:]), "x")), 1)
    input_grad = bf(
        hidden_grad
        + inverse * full
        - inputs * inverse**3 * jnp.mean(full * inputs, axis=-1, keepdims=True)
    )
    scaled = jnp.concatenate(
        [f32(own_cols) * inverse, f32(their_cols) * their_facts[5][:, None]], axis=0
    )
    grad_attn = jnp.sum(normed_grad * scaled, axis=0, keepdims=True)
    grads = [bf(dot_tn(normed, piece)) for piece in pieces]
    return (output, input_grad, grad_attn, grad_ffn, grads, grad_out, grad_gate_up, grad_down)


def apart(values, step, before):
    return lax.optimization_barrier((values, before[step]))[0] if step in before else values


def over_z(part, before):
    chips = lax.axis_size("z")
    if chips != 4:
        return lax.psum(part, "z")
    inner = (lax.axis_index("z") + 1) // 2 == 1
    came = apart(lax.ppermute(part, "z", [(0, 1), (3, 2)]), 1, before)
    held = bf(f32(part) + f32(came))
    came = apart(lax.ppermute(held, "z", [(1, 2), (2, 1)]), 2, before)
    total = bf(f32(held) + f32(came))
    came = apart(lax.ppermute(total, "z", [(1, 0), (2, 3)]), 3, before)
    final = jnp.where(inner, total, came)
    before.update({1: held, 2: total, 3: final})
    return final


def copies(part):
    across = swap(part, "y")
    return [part, swap(part, "c"), across, swap(across, "c")]


def quarter(values):
    for axis in ("c", "y"):
        rows = values.shape[0] // 2
        at = lax.axis_index(axis)
        own = lax.dynamic_slice_in_dim(values, at * rows, rows, 0)
        out = lax.dynamic_slice_in_dim(values, (1 - at) * rows, rows, 0)
        values = bf(f32(own) + f32(swap(out, axis)))
    return values


PIECE = 256


def put_piece(places, parts, whole, rows, block):
    size, width = parts[0].shape
    step = size // 4

    def kernel(places_ref, *refs):
        for flip in range(4):
            refs[-1][places_ref[flip]] = refs[flip][...].astype(jnp.float32)

    part_spec = pl.BlockSpec((step, width), lambda at, places: (at, 0))
    more = [] if whole is None else [whole]
    return pl.pallas_call(
        kernel,
        out_shape=jax.ShapeDtypeStruct((4, rows, width), jnp.float32),
        grid_spec=pltpu.PrefetchScalarGridSpec(
            num_scalar_prefetch=1,
            grid=(4,),
            in_specs=[part_spec] * 4 + [pl.BlockSpec(memory_space=pl.ANY)] * len(more),
            out_specs=pl.BlockSpec(
                (4, step, width), lambda at, places: (0, block * 4 + at, 0)
            ),
        ),
        input_output_aliases={5: 0} if more else {},
    )(places, *parts, *more)


def put_rows(places, parts, widths):
    size, width = parts[0].shape
    step = size // 4

    def kernel(places_ref, *refs):
        for flip in range(4):
            at = 0
            for out, cut in zip(refs[4:], widths):
                out[places_ref[flip]] = refs[flip][:, at : at + cut].astype(jnp.float32)
                at += cut

    outs = pl.pallas_call(
        kernel,
        out_shape=[jax.ShapeDtypeStruct((4, size, cut), jnp.float32) for cut in widths],
        grid_spec=pltpu.PrefetchScalarGridSpec(
            num_scalar_prefetch=1,
            grid=(4,),
            in_specs=[pl.BlockSpec((step, width), lambda at, places: (at, 0))] * 4,
            out_specs=[
                pl.BlockSpec((4, step, cut), lambda at, places: (0, at, 0)) for cut in widths
            ],
        ),
    )(places, *parts)
    return [out.reshape(4 * size, cut) for out, cut in zip(outs, widths)]


def reduced_step(*arrays):
    output, input_grad, grad_attn, grad_ffn, grads, grad_out, grad_gate_up, grad_down = (
        per_device_split(*arrays)
    )
    core, row = lax.axis_index("c"), lax.axis_index("y")
    flips = jnp.arange(4, dtype=jnp.int32)
    experts = (row * 2 + core) ^ flips
    quarters = (core ^ (flips & 1)) * 2 + (row ^ (flips >> 1))
    sums, before = [], {}
    for values in (grad_down, grad_gate_up):
        whole = None
        for at in range(0, values.shape[0], PIECE):
            total = over_z(values[at : at + PIECE], before)
            parts = copies(total)
            rows, block = values.shape[0], at // PIECE
            whole = put_piece(experts, parts, whole, rows, block)
        sums.append(whole)
    sum_down, sum_gate_up = sums

    def over_all(pieces):
        wide = jnp.concatenate(pieces, axis=1)
        parts = copies(over_z(quarter(wide), {}))
        return put_rows(quarters, parts, [p.shape[1] for p in pieces])

    gains = bf(jnp.concatenate([grad_attn, grad_ffn], axis=0)).T
    (sum_out,) = over_all([grad_out])
    *sum_proj, sum_gains = over_all(grads + [jnp.pad(gains, ((0, 0), (0, 126)))])
    return (
        output,
        input_grad,
        sum_gains[:, 0],
        *sum_proj,
        sum_out,
        sum_gains[:, 1],
        sum_gate_up,
        sum_down,
    )


def solution(mesh):
    replicas, shards = mesh.devices.shape
    if shards == 2 and EXPERTS == 8 and replicas % 4 == 0:
        split = jax.sharding.Mesh(
            mesh.devices.reshape(replicas // 4, 2, 2, 2), ("z", "y", "c", "x")
        )
        step = mapped(reduced_step, split, ("z", "y", "c", "x"), "x")
        return step
    return mapped(per_device, mesh, ("rep", "shard"), "shard")


def mapped(step, mesh, every, shard):
    in_specs = (
        P(every, None),
        P(every),
        P(every, None),
        P(every, None),
        P(every, None),
        P(shard),
        P(shard, None),
        P(shard, None),
        P(shard, None),
        P(shard, None),
        P(shard),
        P(shard, None, None),
        P(shard, None, None),
    )
    out_specs = (
        P(every, None),
        P(every, None),
        P(shard),
        P(shard, None),
        P(shard, None),
        P(shard, None),
        P(shard, None),
        P(shard),
        P(shard, None, None),
        P(shard, None, None),
    )
    return jax.shard_map(step, mesh=mesh, in_specs=in_specs, out_specs=out_specs, check_vma=False)
```
